256 devices in a mesh: dp: 32 (over x_lo, z, core), seq: 8 (over x_hi, y).
Axes of the slice: x: 4 (x_hi: 2, x_lo: 2; x = x_hi * 2 + x_lo), y: 4, z: 8, core: 2. Of those that a mesh axis runs over, the one named last changes fastest.
Arguments:
- queries: bfloat16 [32, 1024, 1024], P('dp', 'seq'), may hold values from -6 to 6
- keys: bfloat16 [32, 1024, 1024], P('dp', 'seq'), may hold values from -6 to 6
- values: bfloat16 [32, 1024, 1024], P('dp', 'seq'), may hold values from -6 to 6
- stream: bfloat16 [32, 1024, 1024], P('dp', 'seq'), may hold values from -6 to 6
- cotangent: bfloat16 [32, 1024, 1024], P('dp', 'seq'), may hold values from -6 to 6
- attn_out: bfloat16 [1024, 1024], replicated, may hold values from -0.1875 to 0.1875
- point_in: bfloat16 [1024, 2048], replicated, may hold values from -0.1875 to 0.1875
- kernel: bfloat16 [31, 1024], replicated, may hold values from -1 to 1
- point_out: bfloat16 [1024, 1024], replicated, may hold values from -0.1875 to 0.1875
- norm_gain: float32 [1024], replicated, may hold values from 0.1 to 1.9
- conv_gain: float32 [1024], replicated, may hold values from 0.1 to 1.9
- segments: int32 [32, 1024], replicated, may hold values from 0 to 511, as said below
- plan: int32 [32], replicated, may hold values from 0 to 31, as said below
Outputs:
- query_grad: bfloat16 [32, 1024, 1024], P('dp', 'seq')
- key_grad: bfloat16 [32, 1024, 1024], P('dp', 'seq')
- value_grad: bfloat16 [32, 1024, 1024], P('dp', 'seq')
- stream_grad: bfloat16 [32, 1024, 1024], P('dp', 'seq')
- kernel_grad: float32 [31, 1024], replicated
- proj_grads: float32 [1024, 2048], P(('dp', 'seq'))
The draws below stay inside these ranges and needn't reach their ends.
Inputs may be any that keep to these rules, and one draw needn't show every extreme that they name: `segments`: along each pack the numbers never fall and change only at even frames; one number marks one utterance. `plan`: A permutation of 0 to 31.
All inputs are finite; a program needn't handle non-finite values.
Results may differ from the reference program's by a relative error of at most 0.024.
Values may be sent and summed in bfloat16 or wider, within the bound.
No kernel may reach another device: no remote copies, remote signals or barrier semaphores. Data moves between devices by JAX's collectives and lax.ppermute only.
A program may use at most 128 MiB of HBM per device.

```python
import jax
import jax.numpy as jnp
from jax import lax

D = 1024
HEADS = 16
KERNEL = 31
HEAD_DIM = 64
LENGTH = 1024
PACKS = 32


def draw_queries(key, part):
    fresh = jnp.clip(jax.random.normal(jax.random.fold_in(key, 1), (PACKS, LENGTH, D)), -6.0, 6.0)
    return fresh.astype(jnp.bfloat16)


def draw_keys(key, part):
    fresh = jnp.clip(jax.random.normal(jax.random.fold_in(key, 2), (PACKS, LENGTH, D)), -6.0, 6.0)
    return fresh.astype(jnp.bfloat16)


def draw_segments(key, part):
    level_key, flag_key = jax.random.split(jax.random.fold_in(key, 3))
    level = jax.random.randint(level_key, (PACKS, 1), 0, 4)
    limits = jnp.array([0, 2048, 16384, 131072], jnp.int32)
    thresh = jnp.sum(jnp.where(level == jnp.arange(4)[None, :], limits[None, :], 0), 1, keepdims=True)
    draws = jax.random.randint(flag_key, (PACKS, LENGTH // 2), 0, 1048576)
    flags = (draws < thresh).astype(jnp.int32) * (jnp.arange(LENGTH // 2) > 0).astype(jnp.int32)[None, :]
    pairs = jnp.cumsum(flags, 1).astype(jnp.int32)
    odd = (jnp.arange(PACKS) % 2).astype(jnp.int32)[:, None]
    lift = (LENGTH // 2 - 1 - pairs[:, -1:]) * odd
    return jnp.repeat(pairs + lift, 2, axis=1).astype(jnp.int32)


def draw_plan(key, part):
    return jax.random.permutation(jax.random.fold_in(key, 5), PACKS).astype(jnp.int32)


def shard_levels(stream_key, extent, cuts, smallest, largest):
    factor_of, own = 1.0, jax.random.fold_in(stream_key, 6)
    for axis_at, parts in cuts:
        heights = jnp.exp(jax.random.uniform(jax.random.fold_in(own, axis_at), (parts,), jnp.float32, smallest / len(cuts), largest / len(cuts)))
        factor_of = factor_of * jnp.repeat(heights, extent[axis_at] // parts).reshape([-1 if axis == axis_at else 1 for axis in range(len(extent))])
    return factor_of


def centred(key, dims, deviation, bound, shards=(), held_as=jnp.bfloat16):
    values = deviation * jax.random.normal(key, dims, jnp.float32)
    if shards:
        values = values * shard_levels(key, dims, shards, -0.22, 0.18)
    return jnp.clip(values, -bound, bound).astype(held_as)


def setup_inputs(seed: int = 0) -> dict:
    splits = jax.random.split(jax.random.key(seed), 14)
    queries = draw_queries(jax.random.fold_in(splits[13], 71), 0)
    keys = draw_keys(jax.random.fold_in(splits[13], 71), 0)
    values = centred(splits[2], (PACKS, LENGTH, D), 1.0, 6.0, ((0, 32), (1, 8)))
    stream = centred(splits[3], (PACKS, LENGTH, D), 1.0, 6.0, ((0, 32), (1, 8)))
    cotangent = centred(splits[4], (PACKS, LENGTH, D), 1.0, 6.0, ((0, 32), (1, 8)))
    attn_out = centred(splits[5], (D, D), D ** -0.5, 0.1875)
    point_in = centred(splits[6], (D, 2 * D), D ** -0.5, 0.1875)
    kernel = centred(splits[7], (KERNEL, D), KERNEL ** -0.5, 1.0)
    point_out = centred(splits[8], (D, D), D ** -0.5, 0.1875)
    norm_gain = jnp.clip(1.0 + 0.18 * jax.random.normal(splits[9], (D,), jnp.float32), 0.1, 1.9)
    conv_gain = jnp.clip(1.0 + 0.18 * jax.random.normal(splits[10], (D,), jnp.float32), 0.1, 1.9)
    segments = draw_segments(jax.random.fold_in(splits[13], 71), 0)
    plan = draw_plan(jax.random.fold_in(splits[13], 71), 0)
    return {"queries": queries, "keys": keys, "values": values, "stream": stream, "cotangent": cotangent, "attn_out": attn_out, "point_in": point_in, "kernel": kernel, "point_out": point_out, "norm_gain": norm_gain, "conv_gain": conv_gain, "segments": segments, "plan": plan}


EPSILON = 1e-05
MASKED = -1e+30

def layer_norm(stream, gain):
    center = lax.optimization_barrier(jnp.mean(stream, -1, keepdims=True))
    shifted = stream - center
    inverse = lax.rsqrt(lax.optimization_barrier(jnp.mean(shifted * shifted, -1, keepdims=True)) + EPSILON)
    normed = shifted * inverse
    return (normed * gain, normed, inverse)

def norm_backward(upstream, normed, inverse, gain):
    scaled = upstream * gain
    return inverse * (scaled - lax.optimization_barrier(jnp.mean(scaled, -1, keepdims=True)) - normed * lax.optimization_barrier(jnp.mean(scaled * normed, -1, keepdims=True)))

def swish_slope(values):
    logistic = jax.nn.sigmoid(values)
    return logistic * (1.0 + values * (1.0 - logistic))

def tap_table(padded_ids, own_ids, taps):
    length = own_ids.shape[0]
    return (jnp.stack([padded_ids[tap:tap + length] for tap in range(taps)], 1) == own_ids[:, None]).astype(jnp.float32)

def depthwise(padded, weights, table):
    length = table.shape[0]
    total = jnp.zeros((length, padded.shape[1]), jnp.float32)
    for tap in range(weights.shape[0]):
        total = total + weights[tap].astype(jnp.float32) * padded[tap:tap + length].astype(jnp.float32) * table[:, tap:tap + 1]
    return total

def tap_sums(upstream, padded, table):
    length = table.shape[0]
    return jnp.stack([lax.optimization_barrier(jnp.sum(upstream * padded[tap:tap + length].astype(jnp.float32) * table[:, tap:tap + 1], 0)) for tap in range(table.shape[1])])

def split_heads(matrix):
    return matrix.reshape(matrix.shape[0], HEADS, HEAD_DIM).transpose(1, 0, 2)

def merge_heads(tensor):
    return tensor.transpose(1, 0, 2).reshape(tensor.shape[1], -1)

def head_weights(query_head, key_head, ids):
    scores = jnp.dot(query_head, key_head.T, preferred_element_type=jnp.float32) * HEAD_DIM ** (-0.5)
    scores = jnp.where(ids[:, None] == ids[None, :], scores, MASKED)
    highest = lax.optimization_barrier(jnp.max(scores, -1, keepdims=True))
    log_total = highest + jnp.log(lax.optimization_barrier(jnp.sum(jnp.exp(scores - highest), -1, keepdims=True)))
    return jnp.exp(scores - log_total)

def pack_pass(queries, keys, values, stream, cotangent, ids, attn_out, point_in, kernel, point_out, norm_gain, conv_gain):

    def forward_head(items):
        query_head, key_head, value_head = items
        weights = head_weights(query_head, key_head, ids)
        return jnp.dot(weights.astype(jnp.bfloat16), value_head, preferred_element_type=jnp.float32).astype(jnp.bfloat16)
    query_heads, key_heads, value_heads = (split_heads(queries), split_heads(keys), split_heads(values))
    mixed = merge_heads(lax.map(forward_head, (query_heads, key_heads, value_heads)))
    hidden = stream.astype(jnp.float32) + jnp.dot(mixed, attn_out, preferred_element_type=jnp.float32)
    normed_in, hat_in, inv_in = layer_norm(hidden, norm_gain)
    both = jnp.dot(normed_in.astype(jnp.bfloat16), point_in, preferred_element_type=jnp.float32)
    linear = both[:, :D]
    logistic = jax.nn.sigmoid(both[:, D:])
    conv_in = (linear * logistic).astype(jnp.bfloat16)
    reach = KERNEL // 2
    padded = jnp.pad(conv_in, ((reach, reach), (0, 0)))
    table = tap_table(jnp.pad(ids, reach, constant_values=-1), ids, KERNEL)
    conv_out = depthwise(padded, kernel, table)
    normed_out, hat_out, inv_out = layer_norm(conv_out, conv_gain)
    activated = (normed_out * jax.nn.sigmoid(normed_out)).astype(jnp.bfloat16)
    act_grad = jnp.dot(cotangent, point_out.T, preferred_element_type=jnp.float32)
    conv_grad = norm_backward(act_grad * swish_slope(normed_out), hat_out, inv_out, conv_gain)
    kernel_part = tap_sums(conv_grad, padded, table)
    in_grad = depthwise(jnp.pad(conv_grad, ((reach, reach), (0, 0))), kernel[::-1], table)
    both_grad = jnp.concatenate([in_grad * logistic, in_grad * linear * logistic * (1.0 - logistic)], 1).astype(jnp.bfloat16)
    back_in = jnp.dot(both_grad, point_in.T, preferred_element_type=jnp.float32)
    stream_out = (cotangent.astype(jnp.float32) + norm_backward(back_in, hat_in, inv_in, norm_gain)).astype(jnp.bfloat16)
    mixed_grad = jnp.dot(stream_out, attn_out.T, preferred_element_type=jnp.float32).astype(jnp.bfloat16)
    scale = HEAD_DIM ** (-0.5)

    def backward_head(items):
        query_head, key_head, value_head, grad_head = items
        weights = head_weights(query_head, key_head, ids)
        slope = jnp.dot(grad_head, value_head.T, preferred_element_type=jnp.float32)
        delta = lax.optimization_barrier(jnp.sum(weights * slope, -1, keepdims=True))
        score_grad = (weights * (slope - delta)).astype(jnp.bfloat16)
        query_part = (jnp.dot(score_grad, key_head, preferred_element_type=jnp.float32) * scale).astype(jnp.bfloat16)
        key_part = (jnp.dot(score_grad.T, query_head, preferred_element_type=jnp.float32) * scale).astype(jnp.bfloat16)
        value_part = jnp.dot(weights.astype(jnp.bfloat16).T, grad_head, preferred_element_type=jnp.float32).astype(jnp.bfloat16)
        return (query_part, key_part, value_part)
    query_part, key_part, value_part = lax.map(backward_head, (query_heads, key_heads, value_heads, split_heads(mixed_grad)))
    proj_part = jnp.concatenate([jnp.dot(mixed.T, stream_out, preferred_element_type=jnp.float32), jnp.dot(activated.T, cotangent, preferred_element_type=jnp.float32)], 1)
    return (merge_heads(query_part), merge_heads(key_part), merge_heads(value_part), stream_out, kernel_part, proj_part)

def reference(queries, keys, values, stream, cotangent, attn_out, point_in, kernel, point_out, norm_gain, conv_gain, segments, plan):

    def one_slot(carry, slot):
        source = plan[slot]
        results = pack_pass(queries[source], keys[source], values[source], stream[source], cotangent[source], segments[source], attn_out, point_in, kernel, point_out, norm_gain, conv_gain)
        return ((carry[0] + results[4], carry[1] + results[5]), (results[0], results[1], results[2], results[3]))
    start = (jnp.zeros((KERNEL, D), jnp.float32), jnp.zeros((D, 2 * D), jnp.float32))
    totals, slots = lax.scan(one_slot, start, jnp.arange(PACKS))
    return (slots[0], slots[1], slots[2], slots[3], totals[0], totals[1])
```

```python
import functools

import jax
import jax.numpy as jnp
from jax import lax
from jax.experimental import pallas as pl
from jax.experimental.pallas import tpu as pltpu
from jax.sharding import PartitionSpec as P

HEAD_DIM = 64
EPSILON = 1e-05
MASKED = -1e30
F32 = jnp.float32
BF16 = jnp.bfloat16
HALO = 32
ROWS = 128
WINDOW = ROWS + 2 * HALO
REACH = 15
TAPS = 31

ORDER = (0, 2, 3, 1)


def whole(space=pltpu.VMEM):
    return pl.BlockSpec(memory_space=space)


def across(left, right, dims):
    return lax.dot_general(left, right, (dims, ((), ())), preferred_element_type=F32)


NT = ((1,), (1,))
TN = ((0,), (0,))
NN = ((1,), (0,))


def half_of(matrix, head):
    lanes = lax.broadcasted_iota(jnp.int32, matrix.shape, 1)
    inside = (lanes >= head * HEAD_DIM) & (lanes < (head + 1) * HEAD_DIM)
    return jnp.where(inside, matrix, jnp.zeros_like(matrix))


def pack_kernel(q_ref, k_ref, v_ref, out_ref):
    for head in range(8):
        cols = slice(128 * head, 128 * head + 128)
        out_ref[head, 0] = q_ref[:, cols]
        out_ref[head, 1] = k_ref[:, cols]
        out_ref[head, 2] = v_ref[:, cols]


def pack(queries, keys, values):
    return pl.pallas_call(
        pack_kernel,
        out_shape=jax.ShapeDtypeStruct((8, 3, ROWS, 128), BF16),
        in_specs=[whole()] * 3,
        out_specs=whole(),
        name="pack",
    )(queries, keys, values)


def attend_kernel(qkv_ref, ids_ref, out_ref, weights_ref, id_scratch, mixed_scratch):
    step = pl.program_id(0)

    @pl.when(step == 0)
    def _():
        id_scratch[...] = jnp.broadcast_to(ids_ref[...], (128, 1024)).T
        mixed_scratch[0:HALO, :] = jnp.zeros((HALO, 128), BF16)
        mixed_scratch[1024 + HALO :, :] = jnp.zeros((HALO, 128), BF16)

    keys = qkv_ref[:, 1].reshape(1024, 128)
    values = qkv_ref[:, 2].reshape(1024, 128)
    queries = qkv_ref[pl.ds(2 * step, 2), 0].reshape(256, 128) * jnp.asarray(HEAD_DIM**-0.5, BF16)
    row_ids = ids_ref[:, pl.ds(pl.multiple_of(256 * step, 256), 256)]
    key_ids = id_scratch[...]
    same = jnp.concatenate([key_ids, key_ids], 1) == row_ids
    parts = []
    for head in range(2):
        scores = across(keys, half_of(queries, head), NT)
        scores = jnp.where(same, scores, MASKED)
        highest = jnp.max(scores, 0, keepdims=True)
        raised = jnp.exp(scores - highest)
        total = jnp.sum(raised, 0, keepdims=True)
        weights = (raised * (1.0 / total)).astype(BF16)
        weights_ref[head] = weights
        mixed = across(values, weights, TN)
        parts.append(mixed[64 * head : 64 * head + 64])
    mixed = jnp.concatenate(parts, 0).T.astype(BF16)
    mixed_scratch[pl.ds(pl.multiple_of(HALO + 256 * step, 32), 256), :] = mixed

    @pl.when(step == 3)
    def _():
        for s in range(8):
            out_ref[s] = mixed_scratch[128 * s : 128 * s + WINDOW, :]


def attend(qkv, ids_row):
    return pl.pallas_call(
        attend_kernel,
        grid=(4,),
        out_shape=(
            jax.ShapeDtypeStruct((8, WINDOW, 128), BF16),
            jax.ShapeDtypeStruct((2, 1024, 1024), BF16),
        ),
        in_specs=[
            pl.BlockSpec((8, 3, ROWS, 128), lambda j: (0, 0, 0, 0)),
            pl.BlockSpec((1, 1024), lambda j: (0, 0)),
        ],
        out_specs=(
            pl.BlockSpec((8, WINDOW, 128), lambda j: (0, 0, 0)),
            pl.BlockSpec((2, 1024, 256), lambda j: (0, 0, j)),
        ),
        scratch_shapes=[pltpu.VMEM((1024, 128), F32), pltpu.VMEM((1024 + 2 * HALO, 128), BF16)],
        compiler_params=pltpu.CompilerParams(dimension_semantics=("arbitrary",)),
        name="attend",
    )(qkv, ids_row)


def tap_place(tap):
    return (tap + 1) % 8, (tap + 1) // 8 - 2


def middle_kernel(
    parity_ref,
    mixed_ref,
    stream_ref,
    cotangent_ref,
    before_ref,
    after_ref,
    ids_ref,
    attn_out_ref,
    point_in_ref,
    taps_ref,
    point_out_ref,
    norm_gain_ref,
    conv_gain_ref,
    out_ref,
    keep_ref,
    send_ref,
    conv_in_ref,
    moved_ref,
    grad_ref,
    grad_moved_ref,
    ids_moved_ref,
    taps_f32_ref,
    hat_ref,
    linear_ref,
    logistic_ref,
    act_grad_ref,
    activated_ref,
    in_grad_ref,
):
    own = slice(HALO, HALO + ROWS)
    ids = jnp.broadcast_to(ids_ref[...], (128, 256)).T
    grad_ref[...] = jnp.zeros_like(grad_ref)
    taps_f32_ref[...] = taps_ref[...].astype(F32)
    conv_in_ref[0:8, 0:128] = jnp.zeros((8, 128), F32)
    for m in range(8):
        ids_moved_ref[m] = ids[m : m + WINDOW]

    mixed = jnp.concatenate([mixed_ref[h] for h in range(8)], 1)
    hidden = across(mixed, attn_out_ref[...], NN)
    hidden += jnp.concatenate([before_ref[0:HALO], stream_ref[...], after_ref[0:HALO]], 0).astype(F32)
    center = jnp.mean(hidden, -1, keepdims=True)
    shifted = hidden - center
    inverse = lax.rsqrt(jnp.mean(shifted * shifted, -1, keepdims=True) + EPSILON)
    hat = shifted * inverse
    hat_ref[...] = hat[own]
    inverse_in = inverse[own]
    normed = (hat * norm_gain_ref[...]).astype(BF16)
    for c in range(4):
        cols = slice(256 * c, 256 * c + 256)
        gate_cols = slice(1024 + 256 * c, 1024 + 256 * c + 256)
        linear = across(normed, point_in_ref[:, cols], NN)
        logistic = jax.nn.sigmoid(across(normed, point_in_ref[:, gate_cols], NN))
        conv_in_ref[0:WINDOW, cols] = (linear * logistic).astype(BF16).astype(F32)
        linear_ref[:, cols] = linear[own]
        logistic_ref[:, cols] = logistic[own]

    cotangent = jnp.concatenate(
        [before_ref[HALO : 2 * HALO], cotangent_ref[...], after_ref[HALO : 2 * HALO]], 0
    )
    act_grad_ref[...] = across(cotangent, point_out_ref[...], NT)

    @pl.loop(0, 8)
    def _(block):
        cols = pl.ds(pl.multiple_of(128 * block, 128), 128)
        for m in range(8):
            moved_ref[m, 0:184, cols] = conv_in_ref[m : m + 184, cols]

    conv_gain = conv_gain_ref[...]

    @pl.loop(0, 20)
    def _(group):
        base = pl.multiple_of(16 + 8 * group, 8)
        own_ids = ids_moved_ref[0, pl.ds(base, 8), :]
        sums = [jnp.zeros((8, 128), F32) for _ in range(8)]
        for tap in range(TAPS):
            m, a = tap_place(tap)
            rows = pl.ds(pl.multiple_of(base + 8 * a, 8), 8)
            same = ids_moved_ref[m, rows, :] == own_ids
            for block in range(8):
                cols = slice(128 * block, 128 * block + 128)
                term = jnp.where(same, moved_ref[m, rows, cols], 0.0)
                sums[block] = sums[block] + term * taps_f32_ref[tap : tap + 1, cols]
        conv_out = jnp.concatenate(sums, 1)
        shifted = conv_out - jnp.mean(conv_out, -1, keepdims=True)
        inverse = lax.rsqrt(jnp.mean(shifted * shifted, -1, keepdims=True) + EPSILON)
        hat = shifted * inverse
        normed = hat * conv_gain
        logistic = jax.nn.sigmoid(normed)
        activated_ref[pl.ds(base, 8), :] = normed * logistic
        slope = logistic * (1.0 + normed * (1.0 - logistic))
        scaled = act_grad_ref[pl.ds(base, 8), :] * slope * conv_gain
        grad_ref[pl.ds(base, 8), :] = inverse * (
            scaled
            - jnp.mean(scaled, -1, keepdims=True)
            - hat * jnp.mean(scaled * hat, -1, keepdims=True)
        )

    @pl.loop(0, 8)
    def _(block):
        cols = pl.ds(pl.multiple_of(128 * block, 128), 128)
        for m in range(8):
            grad_moved_ref[m, 0:184, cols] = grad_ref[m : m + 184, cols]

        def row_group(group, tap_sums):
            base = pl.multiple_of(HALO + 8 * group, 8)
            own_ids = ids_moved_ref[0, pl.ds(base, 8), :]
            own_grad = grad_moved_ref[0, pl.ds(base, 8), cols]
            total = jnp.zeros((8, 128), F32)
            sums = []
            for tap in range(TAPS):
                m, a = tap_place(tap)
                rows = pl.ds(pl.multiple_of(base + 8 * a, 8), 8)
                same = ids_moved_ref[m, rows, :] == own_ids
                sums.append(tap_sums[tap] + own_grad * jnp.where(same, moved_ref[m, rows, cols], 0.0))
                back = jnp.where(same, grad_moved_ref[m, rows, cols], 0.0)
                total = total + back * taps_f32_ref[30 - tap : 31 - tap, cols]
            in_grad_ref[pl.ds(pl.multiple_of(8 * group, 8), 8), cols] = total
            return tuple(sums)

        tap_sums = lax.fori_loop(
            0, 16, row_group, tuple(jnp.zeros((8, 128), F32) for _ in range(TAPS))
        )
        rows = [jnp.sum(part, 0, keepdims=True) for part in tap_sums]
        rows.append(jnp.zeros((1, 128), F32))
        out_ref[block, 256:288, :] = jnp.concatenate(rows, 0).astype(BF16)

    back = jnp.zeros((ROWS, 1024), F32)
    for c in range(4):
        cols = slice(256 * c, 256 * c + 256)
        gate_cols = slice(1024 + 256 * c, 1024 + 256 * c + 256)
        logistic = logistic_ref[:, cols]
        toward = in_grad_ref[:, cols] * logistic
        gate = (toward * linear_ref[:, cols] * (1.0 - logistic)).astype(BF16)
        back += across(toward.astype(BF16), point_in_ref[:, cols], NT)
        back += across(gate, point_in_ref[:, gate_cols], NT)
    scaled = back * norm_gain_ref[...]
    hat = hat_ref[...]
    stream_grad = cotangent_ref[...].astype(F32) + inverse_in * (
        scaled
        - jnp.mean(scaled, -1, keepdims=True)
        - hat * jnp.mean(scaled * hat, -1, keepdims=True)
    )
    stream_grad = stream_grad.astype(BF16)
    mixed_grad = across(stream_grad, attn_out_ref[...], NT).astype(BF16)
    for h in range(8):
        cols = slice(128 * h, 128 * h + 128)
        out_ref[h, 0:128, :] = mixed_grad[:, cols]
        out_ref[h, 128:256, :] = stream_grad[:, cols]
    activated = activated_ref[own, :].astype(BF16)
    own_mixed = mixed[own]

    @pl.when(parity_ref[0] == 0)
    def _():
        keep_ref[0:128] = own_mixed
        keep_ref[128:256] = stream_grad
        send_ref[0:128] = activated
        send_ref[128:256] = cotangent_ref[...]

    @pl.when(parity_ref[0] != 0)
    def _():
        keep_ref[0:128] = activated
        keep_ref[128:256] = cotangent_ref[...]
        send_ref[0:128] = own_mixed
        send_ref[128:256] = stream_grad


def middle(parity, *arrays):
    return pl.pallas_call(
        middle_kernel,
        out_shape=(
            jax.ShapeDtypeStruct((8, 288, 128), BF16),
            jax.ShapeDtypeStruct((256, 1024), BF16),
            jax.ShapeDtypeStruct((256, 1024), BF16),
        ),
        in_specs=[whole(pltpu.SMEM)] + [whole()] * 12,
        out_specs=(whole(), whole(), whole()),
        scratch_shapes=[
            pltpu.VMEM((WINDOW, 1024), F32),
            pltpu.VMEM((8, WINDOW, 1024), F32),
            pltpu.VMEM((WINDOW, 1024), F32),
            pltpu.VMEM((8, WINDOW, 1024), F32),
            pltpu.VMEM((8, WINDOW, 128), F32),
            pltpu.VMEM((TAPS, 1024), F32),
            pltpu.VMEM((ROWS, 1024), F32),
            pltpu.VMEM((ROWS, 1024), F32),
            pltpu.VMEM((ROWS, 1024), F32),
            pltpu.VMEM((WINDOW, 1024), F32),
            pltpu.VMEM((WINDOW, 1024), F32),
            pltpu.VMEM((ROWS, 1024), F32),
        ],
        name="middle",
    )(parity, *arrays)


def product_kernel(keep_ref, received_ref, order_ref, out_ref):
    left = jnp.concatenate([keep_ref[0:128], received_ref[0:128]], 0)
    right = jnp.concatenate([keep_ref[128:256], received_ref[128:256]], 0)
    left = across(left, order_ref[...], NN).astype(BF16)
    for c in range(4):
        rows = slice(256 * c, 256 * c + 256)
        out_ref[rows, :] = across(left[:, rows], right, TN).astype(BF16)


def product(keep, received, order):
    return pl.pallas_call(
        product_kernel,
        out_shape=jax.ShapeDtypeStruct((1024, 1024), BF16),
        in_specs=[whole()] * 3,
        out_specs=whole(),
        name="product",
    )(keep, received, order)


def attend_back_kernel(qkv_ref, got_ref, weights_ref, out_ref, dq_ref, dk_ref, dv_ref):
    step = pl.program_id(0)
    keys = qkv_ref[:, 1].reshape(1024, 128)
    values = qkv_ref[:, 2].reshape(1024, 128)
    queries = qkv_ref[pl.ds(2 * step, 2), 0].reshape(256, 128) * jnp.asarray(HEAD_DIM**-0.5, BF16)
    upstream = got_ref[pl.ds(2 * step, 2), 0:128].reshape(256, 128)
    dq_parts = []
    dk_add = jnp.zeros((1024, 128), F32)
    dv_add = jnp.zeros((1024, 128), F32)
    for head in range(2):
        own_up = half_of(upstream, head)
        slope = across(values, own_up, NT)
        weights = weights_ref[head]
        wide = weights.astype(F32)
        delta = jnp.sum(wide * slope, 0, keepdims=True)
        score_grad = (wide * (slope - delta)).astype(BF16)
        dv_add += across(weights, own_up, NN)
        dk_add += across(score_grad, half_of(queries, head), NN)
        dq = across(keys, score_grad, TN)
        dq_parts.append(dq[64 * head : 64 * head + 64])
    dq = jnp.concatenate(dq_parts, 0).T * HEAD_DIM**-0.5
    dq_ref[pl.ds(pl.multiple_of(256 * step, 256), 256), :] = dq.astype(BF16)

    @pl.when(step == 0)
    def _():
        dk_ref[...] = dk_add
        dv_ref[...] = dv_add

    @pl.when(step != 0)
    def _():
        dk_ref[...] += dk_add
        dv_ref[...] += dv_add

    @pl.when(step == 3)
    def _():
        grads = (
            dq_ref[...].reshape(8, 128, 128),
            dk_ref[...].astype(BF16).reshape(8, 128, 128),
            dv_ref[...].astype(BF16).reshape(8, 128, 128),
            got_ref[:, 128:256, :],
        )
        for a in range(4):
            for b in range(8):
                out_ref[8 * a + b, :, 0:16, :] = grads[a][:, 16 * b : 16 * b + 16, :]
        tap_sums = jnp.sum(got_ref[:, 256:288, :].astype(F32), 0)
        for d in range(32):
            row = jnp.broadcast_to(tap_sums[d : d + 1], (8, 128)).astype(BF16)
            out_ref[d, :, 16:24, :] = jnp.broadcast_to(row[None], (8, 8, 128))


def attend_back(qkv, got, weights):
    return pl.pallas_call(
        attend_back_kernel,
        grid=(4,),
        out_shape=jax.ShapeDtypeStruct((32, 8, 24, 128), BF16),
        in_specs=[
            pl.BlockSpec((8, 3, ROWS, 128), lambda j: (0, 0, 0, 0)),
            pl.BlockSpec((8, 288, 128), lambda j: (0, 0, 0)),
            pl.BlockSpec((2, 1024, 256), lambda j: (0, 0, j)),
        ],
        out_specs=pl.BlockSpec((32, 8, 24, 128), lambda j: (0, 0, 0, 0)),
        scratch_shapes=[
            pltpu.VMEM((1024, 128), BF16),
            pltpu.VMEM((1024, 128), F32),
            pltpu.VMEM((1024, 128), F32),
        ],
        compiler_params=pltpu.CompilerParams(dimension_semantics=("arbitrary",)),
        name="attend_back",
    )(qkv, got, weights)


def swap_kernel(plan_ref, got_ref, tail_ref, out_ref):
    parts = []
    for h in range(8):
        parts.append(jnp.sum(got_ref[:, h, 16:24, :].astype(F32), 0))
    tap_row = jnp.concatenate(parts, 1)
    row = lax.broadcasted_iota(jnp.int32, (8, 1024), 0)

    @pl.loop(0, 32)
    def _(slot):
        source = plan_ref[slot]
        for h in range(8):
            out_ref[slot, 0:16, 128 * h : 128 * h + 128] = got_ref[source, h, 0:16, :]
        out_ref[slot, 16:24, :] = jnp.where(row == 4, tap_row, tail_ref[slot]).astype(BF16)


def swap(plan, got, tail):
    return pl.pallas_call(
        swap_kernel,
        out_shape=jax.ShapeDtypeStruct((32, 24, 1024), BF16),
        in_specs=[whole(pltpu.SMEM), whole(), whole()],
        out_specs=whole(),
        name="swap",
    )(plan, got, tail)


def unpack_kernel(got_ref, dq_ref, dk_ref, dv_ref, stream_ref, taps_ref, proj_ref):
    outs = (dq_ref, dk_ref, dv_ref, stream_ref)
    for a in range(4):
        for b in range(8):
            outs[a][16 * b : 16 * b + 16, :] = got_ref[8 * a + b, 0:16, :]
    first = jnp.zeros((8, 1024), F32)
    second = jnp.zeros((8, 1024), F32)
    for d in range(32):
        tail = got_ref[d, 16:24, :].astype(F32)
        if d < TAPS:
            taps_ref[d : d + 1, :] = tail[4:5]
        if d % 2 == 0:
            first += tail
        else:
            second += tail
    proj_ref[:, 0:1024] = first[0:4]
    proj_ref[:, 1024:2048] = second[0:4]


def unpack(got):
    rows = jax.ShapeDtypeStruct((ROWS, 1024), BF16)
    return pl.pallas_call(
        unpack_kernel,
        out_shape=(
            rows,
            rows,
            rows,
            rows,
            jax.ShapeDtypeStruct((TAPS, 1024), F32),
            jax.ShapeDtypeStruct((4, 2048), F32),
        ),
        in_specs=[whole()],
        out_specs=(whole(),) * 6,
        name="unpack",
    )(got)


def spread(array, axis):
    return lax.all_to_all(array, axis, split_axis=0, concat_axis=0, tiled=True)


def place_of(s):
    y = s % 4
    return jnp.where(y == 0, 0, jnp.where(y == 3, 1, jnp.where(y == 1, 2, 3)))


def halve(kept, half, partner):
    size = kept.shape[0] // 2
    sent = lax.dynamic_slice_in_dim(kept, (1 - half) * size, size).astype(BF16)
    mine = lax.dynamic_slice_in_dim(kept, half * size, size).astype(F32)
    return mine + lax.ppermute(sent, "seq", partner).astype(F32)


def per_device(
    queries,
    keys,
    values,
    stream,
    cotangent,
    attn_out,
    point_in,
    kernel,
    point_out,
    norm_gain,
    conv_gain,
    segments,
    plan,
):
    queries, keys, values, stream, cotangent = (
        array[0] for array in (queries, keys, values, stream, cotangent)
    )
    slot = lax.axis_index("dp")
    place = lax.axis_index("seq")
    ids = lax.dynamic_index_in_dim(segments, slot, 0, keepdims=False).astype(F32)
    ids_window = lax.dynamic_slice_in_dim(
        jnp.pad(ids, (HALO, 256 - ROWS - HALO), constant_values=-1.0), place * ROWS, 256
    )
    before = lax.ppermute(
        jnp.concatenate([stream[-HALO:], cotangent[-HALO:]], 0),
        "seq",
        [(i, i + 1) for i in range(7)],
    )
    after = lax.ppermute(
        jnp.concatenate([stream[:HALO], cotangent[:HALO]], 0),
        "seq",
        [(i + 1, i) for i in range(7)],
    )
    qkv = spread(pack(queries, keys, values), "seq")
    mixed_heads, weights = attend(qkv, ids[None])
    mixed = spread(mixed_heads, "seq")
    outgoing, keep, send = middle(
        lax.rem(slot, 2)[None].astype(jnp.int32),
        mixed,
        stream,
        cotangent,
        before,
        after,
        ids_window[None],
        attn_out,
        point_in,
        kernel,
        point_out,
        norm_gain[None],
        conv_gain[None],
    )
    got = spread(outgoing, "seq")
    received = lax.ppermute(send, "dp", [(i, i ^ 1) for i in range(32)])
    row = lax.broadcasted_iota(jnp.int32, (1024, 1024), 0)
    column = lax.broadcasted_iota(jnp.int32, (1024, 1024), 1)
    seq_of = (row % 32) // 4
    goal = 512 * (seq_of // 4) + 128 * place_of(seq_of) + 4 * (row // 32) + row % 4
    order = (column == goal).astype(BF16)
    summed = product(keep, received, order)
    y_place = place_of(place)
    summed = halve(summed, place // 4, [(i, i ^ 4) for i in range(8)])
    summed = halve(summed, y_place // 2, [(i, i ^ 1) for i in range(8)])
    summed = halve(summed, y_place % 2, [(i, (i & 4) | (3 - (i & 3))) for i in range(8)])
    tail = jnp.pad(summed.reshape(32, 4, 1024), ((0, 0), (0, 4), (0, 0)))

    first = attend_back(qkv, got, weights)
    first = spread(first.reshape(256, 24, 128), ("dp", "seq")).reshape(32, 8, 24, 128)
    second = spread(swap(plan, first, tail), "dp")
    dq, dk, dv, stream_grad, kernel_grad, proj_grads = unpack(second)
    return (dq[None], dk[None], dv[None], stream_grad[None], kernel_grad, proj_grads)


def solution(mesh):
    rows = P("dp", "seq", None)
    return jax.shard_map(
        per_device,
        mesh=mesh,
        in_specs=(rows,) * 5 + (P(),) * 8,
        out_specs=(rows, rows, rows, rows, P(), P(("dp", "seq"), None)),
        check_vma=False,
    )
```

```python
import jax
import jax.numpy as jnp
from jax import lax
from jax.experimental import pallas as pl
from jax.experimental.pallas import tpu as pltpu
from jax.sharding import PartitionSpec as P


HEAD_DIM = 64
EPSILON = 1e-05
MASKED = -1e30
F32 = jnp.float32
BF16 = jnp.bfloat16
HALO = 32
ROWS = 128
WINDOW = ROWS + 2 * HALO
TAPS = 31


def whole(space=pltpu.VMEM):
    return pl.BlockSpec(memory_space=space)


def in_hbm(shape, dtype):
    return pltpu.HBM(shape, dtype)


def from_hbm(array):
    return pltpu.with_memory_space_constraint(array, pltpu.HBM)


def across(left, right, dims):
    return lax.dot_general(left, right, (dims, ((), ())), preferred_element_type=F32)


NT = ((1,), (1,))
TN = ((0,), (0,))
NN = ((1,), (0,))


def half_of(matrix, head):
    lanes = lax.broadcasted_iota(jnp.int32, matrix.shape, 1)
    inside = (lanes >= head * HEAD_DIM) & (lanes < (head + 1) * HEAD_DIM)
    return jnp.where(inside, matrix, jnp.zeros_like(matrix))


def pack_kernel(q_ref, k_ref, v_ref, out_ref):
    for head in range(8):
        cols = slice(128 * head, 128 * head + 128)
        out_ref[head, 0] = q_ref[:, cols]
        out_ref[head, 1] = k_ref[:, cols]
        out_ref[head, 2] = v_ref[:, cols]


def pack(queries, keys, values):
    return pl.pallas_call(
        pack_kernel,
        out_shape=in_hbm((8, 3, ROWS, 128), BF16),
        in_specs=[whole()] * 3,
        out_specs=whole(),
        compiler_params=pltpu.CompilerParams(vmem_limit_bytes=6 << 20),
        name="pack",
    )(from_hbm(queries), from_hbm(keys), from_hbm(values))


def attend_kernel(qkv_ref, ids_ref, out_ref, weights_ref, id_scratch, mixed_scratch):
    step = pl.program_id(0)

    @pl.when(step == 0)
    def _():
        id_scratch[...] = jnp.broadcast_to(ids_ref[...], (128, 1024)).T
        mixed_scratch[0:HALO, :] = jnp.zeros((HALO, 128), BF16)
        mixed_scratch[1024 + HALO :, :] = jnp.zeros((HALO, 128), BF16)

    keys = qkv_ref[:, 1].reshape(1024, 128)
    values = qkv_ref[:, 2].reshape(1024, 128)
    queries = qkv_ref[pl.ds(2 * step, 2), 0].reshape(256, 128) * jnp.asarray(HEAD_DIM**-0.5, BF16)
    row_ids = ids_ref[:, pl.ds(pl.multiple_of(256 * step, 256), 256)]
    key_ids = id_scratch[...]
    same = jnp.concatenate([key_ids, key_ids], 1) == row_ids
    parts = []
    for head in range(2):
        scores = across(keys, half_of(queries, head), NT)
        scores = jnp.where(same, scores, MASKED)
        highest = jnp.max(scores, 0, keepdims=True)
        raised = jnp.exp(scores - highest)
        total = jnp.sum(raised, 0, keepdims=True)
        weights = (raised * (1.0 / total)).astype(BF16)
        weights_ref[head] = weights
        mixed = across(values, weights, TN)
        parts.append(mixed[64 * head : 64 * head + 64])
    mixed = jnp.concatenate(parts, 0).T.astype(BF16)
    mixed_scratch[pl.ds(pl.multiple_of(HALO + 256 * step, 32), 256), :] = mixed

    @pl.when(step == 3)
    def _():
        for s in range(8):
            out_ref[s] = mixed_scratch[128 * s : 128 * s + WINDOW, :]


def attend(qkv, ids_row):
    return pl.pallas_call(
        attend_kernel,
        grid=(4,),
        out_shape=(
            in_hbm((8, WINDOW, 128), BF16),
            in_hbm((2, 1024, 1024), BF16),
        ),
        in_specs=[
            pl.BlockSpec((8, 3, ROWS, 128), lambda j: (0, 0, 0, 0)),
            pl.BlockSpec((1, 1024), lambda j: (0, 0)),
        ],
        out_specs=(
            pl.BlockSpec((8, WINDOW, 128), lambda j: (0, 0, 0)),
            pl.BlockSpec((2, 1024, 256), lambda j: (0, 0, j)),
        ),
        scratch_shapes=[pltpu.VMEM((1024, 128), F32), pltpu.VMEM((1024 + 2 * HALO, 128), BF16)],
        compiler_params=pltpu.CompilerParams(
            dimension_semantics=("arbitrary",), vmem_limit_bytes=20 << 20
        ),
        name="attend",
    )(qkv, ids_row)


def tap_place(tap):
    return (tap + 1) % 8, (tap + 1) // 8 - 2


def middle_kernel(
    parity_ref,
    mixed_ref,
    stream_ref,
    cotangent_ref,
    before_ref,
    after_ref,
    ids_ref,
    attn_out_hbm,
    point_in_hbm,
    taps_ref,
    point_out_hbm,
    norm_gain_ref,
    conv_gain_ref,
    out_ref,
    keep_ref,
    send_ref,
    attn_out_ref,
    point_in_ref,
    point_out_ref,
    arrivals,
    conv_in_ref,
    moved_ref,
    grad_ref,
    grad_moved_ref,
    ids_moved_ref,
    taps_f32_ref,
    hat_ref,
    linear_ref,
    logistic_ref,
    act_grad_ref,
    activated_ref,
    in_grad_ref,
):
    own = slice(HALO, HALO + ROWS)
    attn_out_copy = pltpu.make_async_copy(attn_out_hbm, attn_out_ref, arrivals.at[0])
    point_in_copy = pltpu.make_async_copy(point_in_hbm, point_in_ref, arrivals.at[1])
    point_out_copy = pltpu.make_async_copy(point_out_hbm, point_out_ref, arrivals.at[2])
    attn_out_copy.start()
    point_in_copy.start()
    point_out_copy.start()
    ids = jnp.broadcast_to(ids_ref[...], (128, 256)).T
    grad_ref[...] = jnp.zeros_like(grad_ref)
    taps_f32_ref[...] = taps_ref[...].astype(F32)
    conv_in_ref[0:8, 0:128] = jnp.zeros((8, 128), F32)
    for m in range(8):
        ids_moved_ref[m] = ids[m : m + WINDOW]

    mixed = jnp.concatenate([mixed_ref[h] for h in range(8)], 1)
    attn_out_copy.wait()
    hidden = across(mixed, attn_out_ref[...], NN)
    hidden += jnp.concatenate([before_ref[0:HALO], stream_ref[...], after_ref[0:HALO]], 0).astype(F32)
    center = jnp.mean(hidden, -1, keepdims=True)
    shifted = hidden - center
    inverse = lax.rsqrt(jnp.mean(shifted * shifted, -1, keepdims=True) + EPSILON)
    hat = shifted * inverse
    hat_ref[...] = hat[own]
    inverse_in = inverse[own]
    normed = (hat * norm_gain_ref[...]).astype(BF16)
    point_in_copy.wait()
    for c in range(4):
        cols = slice(256 * c, 256 * c + 256)
        gate_cols = slice(1024 + 256 * c, 1024 + 256 * c + 256)
        linear = across(normed, point_in_ref[:, cols], NN)
        logistic = jax.nn.sigmoid(across(normed, point_in_ref[:, gate_cols], NN))
        conv_in_ref[0:WINDOW, cols] = (linear * logistic).astype(BF16).astype(F32)
        linear_ref[:, cols] = linear[own]
        logistic_ref[:, cols] = logistic[own]

    cotangent = jnp.concatenate(
        [before_ref[HALO : 2 * HALO], cotangent_ref[...], after_ref[HALO : 2 * HALO]], 0
    )
    point_out_copy.wait()
    act_grad_ref[...] = across(cotangent, point_out_ref[...], NT)

    @pl.loop(0, 8)
    def _(block):
        cols = pl.ds(pl.multiple_of(128 * block, 128), 128)
        for m in range(8):
            moved_ref[m, 0:184, cols] = conv_in_ref[m : m + 184, cols]

    conv_gain = conv_gain_ref[...]

    @pl.loop(0, 20)
    def _(group):
        base = pl.multiple_of(16 + 8 * group, 8)
        own_ids = ids_moved_ref[0, pl.ds(base, 8), :]
        sums = [jnp.zeros((8, 128), F32) for _ in range(8)]
        for tap in range(TAPS):
            m, a = tap_place(tap)
            rows = pl.ds(pl.multiple_of(base + 8 * a, 8), 8)
            same = ids_moved_ref[m, rows, :] == own_ids
            for block in range(8):
                cols = slice(128 * block, 128 * block + 128)
                term = jnp.where(same, moved_ref[m, rows, cols], 0.0)
                sums[block] = sums[block] + term * taps_f32_ref[tap : tap + 1, cols]
        conv_out = jnp.concatenate(sums, 1)
        shifted = conv_out - jnp.mean(conv_out, -1, keepdims=True)
        inverse = lax.rsqrt(jnp.mean(shifted * shifted, -1, keepdims=True) + EPSILON)
        hat = shifted * inverse
        normed = hat * conv_gain
        logistic = jax.nn.sigmoid(normed)
        activated_ref[pl.ds(base, 8), :] = normed * logistic
        slope = logistic * (1.0 + normed * (1.0 - logistic))
        scaled = act_grad_ref[pl.ds(base, 8), :] * slope * conv_gain
        grad_ref[pl.ds(base, 8), :] = inverse * (
            scaled
            - jnp.mean(scaled, -1, keepdims=True)
            - hat * jnp.mean(scaled * hat, -1, keepdims=True)
        )

    @pl.loop(0, 8)
    def _(block):
        cols = pl.ds(pl.multiple_of(128 * block, 128), 128)
        for m in range(8):
            grad_moved_ref[m, 0:184, cols] = grad_ref[m : m + 184, cols]

        def row_group(group, tap_sums):
            base = pl.multiple_of(HALO + 8 * group, 8)
            own_ids = ids_moved_ref[0, pl.ds(base, 8), :]
            own_grad = grad_moved_ref[0, pl.ds(base, 8), cols]
            total = jnp.zeros((8, 128), F32)
            sums = []
            for tap in range(TAPS):
                m, a = tap_place(tap)
                rows = pl.ds(pl.multiple_of(base + 8 * a, 8), 8)
                same = ids_moved_ref[m, rows, :] == own_ids
                sums.append(tap_sums[tap] + own_grad * jnp.where(same, moved_ref[m, rows, cols], 0.0))
                back = jnp.where(same, grad_moved_ref[m, rows, cols], 0.0)
                total = total + back * taps_f32_ref[30 - tap : 31 - tap, cols]
            in_grad_ref[pl.ds(pl.multiple_of(8 * group, 8), 8), cols] = total
            return tuple(sums)

        tap_sums = lax.fori_loop(
            0, 16, row_group, tuple(jnp.zeros((8, 128), F32) for _ in range(TAPS))
        )
        rows = [jnp.sum(part, 0, keepdims=True) for part in tap_sums]
        rows.append(jnp.zeros((1, 128), F32))
        tap_part = jnp.concatenate(rows, 0).astype(BF16)
        keep_ref[256:288, cols] = tap_part
        send_ref[256:288, cols] = tap_part

    back = jnp.zeros((ROWS, 1024), F32)
    for c in range(4):
        cols = slice(256 * c, 256 * c + 256)
        gate_cols = slice(1024 + 256 * c, 1024 + 256 * c + 256)
        logistic = logistic_ref[:, cols]
        toward = in_grad_ref[:, cols] * logistic
        gate = (toward * linear_ref[:, cols] * (1.0 - logistic)).astype(BF16)
        back += across(toward.astype(BF16), point_in_ref[:, cols], NT)
        back += across(gate, point_in_ref[:, gate_cols], NT)
    scaled = back * norm_gain_ref[...]
    hat = hat_ref[...]
    stream_grad = cotangent_ref[...].astype(F32) + inverse_in * (
        scaled
        - jnp.mean(scaled, -1, keepdims=True)
        - hat * jnp.mean(scaled * hat, -1, keepdims=True)
    )
    stream_grad = stream_grad.astype(BF16)
    mixed_grad = across(stream_grad, attn_out_ref[...], NT).astype(BF16)
    for h in range(8):
        cols = slice(128 * h, 128 * h + 128)
        out_ref[h, 0:128, :] = mixed_grad[:, cols]
        out_ref[h, 128:256, :] = stream_grad[:, cols]
    activated = activated_ref[own, :].astype(BF16)
    own_mixed = mixed[own]

    @pl.when(parity_ref[0] == 0)
    def _():
        keep_ref[0:128] = own_mixed
        keep_ref[128:256] = stream_grad
        send_ref[0:128] = activated
        send_ref[128:256] = cotangent_ref[...]

    @pl.when(parity_ref[0] != 0)
    def _():
        keep_ref[0:128] = activated
        keep_ref[128:256] = cotangent_ref[...]
        send_ref[0:128] = own_mixed
        send_ref[128:256] = stream_grad


def middle(parity, *arrays):
    return pl.pallas_call(
        middle_kernel,
        out_shape=(
            in_hbm((8, 256, 128), BF16),
            in_hbm((288, 1024), BF16),
            in_hbm((288, 1024), BF16),
        ),
        in_specs=[whole(pltpu.SMEM)]
        + [whole()] * 6
        + [whole(pl.ANY), whole(pl.ANY), whole(), whole(pl.ANY), whole(), whole()],
        out_specs=(whole(), whole(), whole()),
        scratch_shapes=[
            pltpu.VMEM((1024, 1024), BF16),
            pltpu.VMEM((1024, 2048), BF16),
            pltpu.VMEM((1024, 1024), BF16),
            pltpu.SemaphoreType.DMA((3,)),
            pltpu.VMEM((WINDOW, 1024), F32),
            pltpu.VMEM((8, WINDOW, 1024), F32),
            pltpu.VMEM((WINDOW, 1024), F32),
            pltpu.VMEM((8, WINDOW, 1024), F32),
            pltpu.VMEM((8, WINDOW, 128), F32),
            pltpu.VMEM((TAPS, 1024), F32),
            pltpu.VMEM((ROWS, 1024), F32),
            pltpu.VMEM((ROWS, 1024), F32),
            pltpu.VMEM((ROWS, 1024), F32),
            pltpu.VMEM((WINDOW, 1024), F32),
            pltpu.VMEM((WINDOW, 1024), F32),
            pltpu.VMEM((ROWS, 1024), F32),
        ],
        compiler_params=pltpu.CompilerParams(vmem_limit_bytes=40 << 20),
        name="middle",
    )(parity, *arrays)


def product_kernel(place_ref, keep_ref, received_ref, own_ref, *out_refs):
    taps_ref = out_refs[7]
    left = jnp.concatenate([keep_ref[0:128], received_ref[0:128]], 0)
    right = jnp.concatenate([keep_ref[128:256], received_ref[128:256]], 0)
    row = lax.broadcasted_iota(jnp.int32, (1024, 128), 0)
    block = ((row & 31) >> 2) ^ place_ref[0]
    goal = 128 * block + 4 * (row >> 5) + (row & 3)
    lane = lax.broadcasted_iota(jnp.int32, (1024, 128), 1)
    for c in range(4):
        order = jnp.concatenate(
            [
                jnp.where(goal == lane + (256 * c + 128 * e), 1.0, 0.0).astype(BF16)
                for e in range(2)
            ],
            1,
        )
        ordered = across(left, order, NN).astype(BF16)
        result = across(ordered, right, TN)
        if c == 0:
            own_ref[...] = result[0:128]
        else:
            out_refs[2 * c - 1][...] = result[0:128].astype(BF16)
        out_refs[2 * c][...] = result[128:256].astype(BF16)
    taps_ref[...] = keep_ref[256:288].astype(F32) + received_ref[256:288].astype(F32)


def product(place, keep, received):
    return pl.pallas_call(
        product_kernel,
        out_shape=(
            jax.ShapeDtypeStruct((ROWS, 1024), F32),
            *(in_hbm((ROWS, 1024), BF16) for _ in range(7)),
            in_hbm((32, 1024), F32),
        ),
        in_specs=[whole(pltpu.SMEM), whole(), whole()],
        out_specs=(whole(),) * 9,
        compiler_params=pltpu.CompilerParams(vmem_limit_bytes=14 << 20),
        name="product",
    )(place, keep, received)


def attend_back_kernel(qkv_ref, got_ref, weights_ref, out_ref, dq_ref, dk_ref, dv_ref):
    step = pl.program_id(0)
    keys = qkv_ref[:, 1].reshape(1024, 128)
    values = qkv_ref[:, 2].reshape(1024, 128)
    queries = qkv_ref[pl.ds(2 * step, 2), 0].reshape(256, 128) * jnp.asarray(HEAD_DIM**-0.5, BF16)
    upstream = got_ref[pl.ds(2 * step, 2), 0:128].reshape(256, 128)
    dq_parts = []
    dk_add = jnp.zeros((1024, 128), F32)
    dv_add = jnp.zeros((1024, 128), F32)
    for head in range(2):
        own_up = half_of(upstream, head)
        slope = across(values, own_up, NT)
        weights = weights_ref[head]
        wide = weights.astype(F32)
        delta = jnp.sum(wide * slope, 0, keepdims=True)
        score_grad = (wide * (slope - delta)).astype(BF16)
        dv_add += across(weights, own_up, NN)
        dk_add += across(score_grad, half_of(queries, head), NN)
        dq = across(keys, score_grad, TN)
        dq_parts.append(dq[64 * head : 64 * head + 64])
    dq = jnp.concatenate(dq_parts, 0).T * HEAD_DIM**-0.5
    dq_ref[pl.ds(pl.multiple_of(256 * step, 256), 256), :] = dq.astype(BF16)

    @pl.when(step == 0)
    def _():
        dk_ref[...] = dk_add
        dv_ref[...] = dv_add

    @pl.when(step != 0)
    def _():
        dk_ref[...] += dk_add
        dv_ref[...] += dv_add

    @pl.when(step == 3)
    def _():
        grads = (
            dq_ref[...].reshape(8, 128, 128),
            dk_ref[...].astype(BF16).reshape(8, 128, 128),
            dv_ref[...].astype(BF16).reshape(8, 128, 128),
            got_ref[:, 128:256, :],
        )
        for a in range(4):
            for b in range(8):
                out_ref[8 * a + b] = grads[a][:, 16 * b : 16 * b + 16, :]


def attend_back(qkv, got, weights):
    return pl.pallas_call(
        attend_back_kernel,
        grid=(4,),
        out_shape=in_hbm((32, 8, 16, 128), BF16),
        in_specs=[
            pl.BlockSpec((8, 3, ROWS, 128), lambda j: (0, 0, 0, 0)),
            pl.BlockSpec((8, 256, 128), lambda j: (0, 0, 0)),
            pl.BlockSpec((2, 1024, 256), lambda j: (0, 0, j)),
        ],
        out_specs=pl.BlockSpec((32, 8, 16, 128), lambda j: (0, 0, 0, 0)),
        scratch_shapes=[
            pltpu.VMEM((1024, 128), BF16),
            pltpu.VMEM((1024, 128), F32),
            pltpu.VMEM((1024, 128), F32),
        ],
        compiler_params=pltpu.CompilerParams(
            dimension_semantics=("arbitrary",), vmem_limit_bytes=20 << 20
        ),
        name="attend_back",
    )(qkv, got, from_hbm(weights))


def swap_kernel(plan_ref, got_ref, tail_ref, out_ref):
    @pl.loop(0, 32)
    def _(slot):
        source = plan_ref[slot]
        for h in range(8):
            out_ref[slot, 16 * h : 16 * h + 16, :] = got_ref[source, h]
        rows = tail_ref[slot]
        pieces = [rows[0:4, 128 * c : 128 * c + 128] for c in range(8)]
        out_ref[slot, 128:160, :] = jnp.concatenate(pieces, 0).astype(BF16)


def swap(plan, got, tail):
    return pl.pallas_call(
        swap_kernel,
        out_shape=in_hbm((32, 160, 128), BF16),
        in_specs=[whole(pltpu.SMEM), whole(), whole()],
        out_specs=whole(),
        compiler_params=pltpu.CompilerParams(vmem_limit_bytes=6 << 20),
        name="swap",
    )(plan, got, tail)


def unpack_kernel(got_ref, dq_ref, dk_ref, dv_ref, stream_ref, proj_ref):
    outs = (dq_ref, dk_ref, dv_ref, stream_ref)
    for a in range(4):
        for b in range(8):
            for h in range(8):
                outs[a][16 * b : 16 * b + 16, 128 * h : 128 * h + 128] = got_ref[
                    8 * a + b, 16 * h : 16 * h + 16, :
                ]
    for core in range(2):
        total = jnp.zeros((32, 128), F32)
        for chip in range(16):
            total += got_ref[2 * chip + core, 128:160, :].astype(F32)
        for c in range(8):
            at = 1024 * core + 128 * c
            proj_ref[:, at : at + 128] = total[4 * c : 4 * c + 4]


def unpack(got):
    rows = jax.ShapeDtypeStruct((ROWS, 1024), BF16)
    return pl.pallas_call(
        unpack_kernel,
        out_shape=(rows, rows, rows, rows, jax.ShapeDtypeStruct((4, 2048), F32)),
        in_specs=[whole()],
        out_specs=(whole(),) * 5,
        compiler_params=pltpu.CompilerParams(vmem_limit_bytes=6 << 20),
        name="unpack",
    )(got)


def spread(array, axis):
    return lax.all_to_all(array, axis, split_axis=0, concat_axis=0, tiled=True)


def add_from(taps, axis, partner):
    arrived = lax.ppermute(taps, axis, partner)
    return taps + arrived


def per_device(
    queries,
    keys,
    values,
    stream,
    cotangent,
    attn_out,
    point_in,
    kernel,
    point_out,
    norm_gain,
    conv_gain,
    segments,
    plan,
):
    queries, keys, values, stream, cotangent = (
        array[0] for array in (queries, keys, values, stream, cotangent)
    )
    slot = lax.axis_index("dp")
    place = lax.axis_index("seq")
    ids = lax.dynamic_index_in_dim(segments, slot, 0, keepdims=False).astype(F32)
    ids_window = lax.dynamic_slice_in_dim(
        jnp.pad(ids, (HALO, 256 - ROWS - HALO), constant_values=-1.0), place * ROWS, 256
    )
    before = lax.ppermute(
        jnp.concatenate([stream[-HALO:], cotangent[-HALO:]], 0),
        "seq",
        [(i, i + 1) for i in range(7)],
    )
    after = lax.ppermute(
        jnp.concatenate([stream[:HALO], cotangent[:HALO]], 0),
        "seq",
        [(i + 1, i) for i in range(7)],
    )
    qkv = spread(pack(queries, keys, values), "seq")
    mixed_heads, weights = attend(qkv, ids[None])
    mixed = spread(mixed_heads, "seq")
    outgoing, keep, send = middle(
        lax.rem(slot, 2)[None].astype(jnp.int32),
        mixed,
        stream,
        cotangent,
        before,
        after,
        ids_window[None],
        from_hbm(attn_out),
        from_hbm(point_in),
        kernel,
        from_hbm(point_out),
        norm_gain[None],
        conv_gain[None],
    )
    got = spread(outgoing, "seq")
    received = lax.ppermute(send, "dp", [(i, i ^ 1) for i in range(32)])
    own, *parts, taps = product(place[None].astype(jnp.int32), keep, received)
    taps = add_from(taps, "dp", [(i, i ^ 2) for i in range(32)])
    taps = add_from(taps, "dp", [(i, i ^ 4) for i in range(32)])
    arrived = [
        lax.ppermute(part, "seq", [(i, i ^ (k + 1)) for i in range(8)])
        for k, part in enumerate(parts)
    ]
    taps = add_from(taps, "dp", [(i, i ^ 8) for i in range(32)])
    first = attend_back(qkv, got, weights)
    first = spread(first.reshape(256, 16, 128), ("dp", "seq"))
    first = first.reshape(32, 8, 16, 128)
    for part in arrived:
        own = own + part.astype(F32)
    tail = jnp.pad(own.reshape(32, 4, 1024), ((0, 0), (0, 4), (0, 0)))
    taps = add_from(taps, "dp", [(i, i ^ 16) for i in range(32)])

    second, taps = lax.optimization_barrier((swap(plan, first, tail), taps))
    for bit in (4, 1, 2):
        taps = add_from(taps, "seq", [(i, i ^ bit) for i in range(8)])
    second = spread(second, "dp")
    dq, dk, dv, stream_grad, proj_grads = unpack(second)
    return (dq[None], dk[None], dv[None], stream_grad[None], taps[:TAPS], proj_grads)


def solution(mesh):
    rows = P("dp", "seq", None)

    return jax.shard_map(
        per_device,
        mesh=mesh,
        in_specs=(rows,) * 5 + (P(),) * 8,
        out_specs=(rows, rows, rows, rows, P(), P(("dp", "seq"), None)),
        check_vma=False,
    )
```

```python
import jax
import jax.numpy as jnp
from jax import lax
from jax.experimental import pallas as pl
from jax.experimental.pallas import tpu as pltpu
from jax.sharding import PartitionSpec as P


HEAD_DIM = 64
EPSILON = 1e-05
MASKED = -1e30
F32 = jnp.float32
BF16 = jnp.bfloat16
HALO = 32
ROWS = 128
WINDOW = ROWS + 2 * HALO
TAPS = 31


def whole(space=pltpu.VMEM):
    return pl.BlockSpec(memory_space=space)


def in_hbm(shape, dtype):
    return pltpu.HBM(shape, dtype)


def from_hbm(array):
    return pltpu.with_memory_space_constraint(array, pltpu.HBM)


def across(left, right, dims):
    return lax.dot_general(left, right, (dims, ((), ())), preferred_element_type=F32)


NT = ((1,), (1,))
TN = ((0,), (0,))
NN = ((1,), (0,))


def half_of(matrix, head):
    lanes = lax.broadcasted_iota(jnp.int32, matrix.shape, 1)
    inside = (lanes >= head * HEAD_DIM) & (lanes < (head + 1) * HEAD_DIM)
    return jnp.where(inside, matrix, jnp.zeros_like(matrix))


def pack_kernel(q_ref, k_ref, v_ref, out_ref):
    for head in range(8):
        cols = slice(128 * head, 128 * head + 128)
        out_ref[head, 0] = q_ref[:, cols]
        out_ref[head, 1] = k_ref[:, cols]
        out_ref[head, 2] = v_ref[:, cols]


def pack(queries, keys, values):
    return pl.pallas_call(
        pack_kernel,
        out_shape=in_hbm((8, 3, ROWS, 128), BF16),
        in_specs=[whole()] * 3,
        out_specs=whole(),
        compiler_params=pltpu.CompilerParams(vmem_limit_bytes=6 << 20),
        name="pack",
    )(from_hbm(queries), from_hbm(keys), from_hbm(values))


def attend_kernel(
    qkv_ref, ids_ref, out_ref, weights_ref, id_scratch, mixed_scratch, turned_scratch, score_scratch
):
    step = pl.program_id(0)

    @pl.when(step == 0)
    def _():
        id_scratch[...] = jnp.broadcast_to(ids_ref[...], (128, 1024)).T
        mixed_scratch[0:HALO, :] = jnp.zeros((HALO, 128), BF16)
        mixed_scratch[1024 + HALO :, :] = jnp.zeros((HALO, 128), BF16)
        turned_scratch[...] = qkv_ref[:, 2].reshape(1024, 128).T

    queries = qkv_ref[pl.ds(2 * step, 2), 0].reshape(256, 128) * jnp.asarray(HEAD_DIM**-0.5, BF16)
    row_ids = ids_ref[:, pl.ds(pl.multiple_of(256 * step, 256), 256)]
    peaks = []
    for head in range(2):
        own_queries = half_of(queries, head)
        peak = jnp.full((8, 256), MASKED, F32)
        for i in range(8):
            rows = slice(128 * i, 128 * i + 128)
            key_ids = id_scratch[rows, :]
            same = jnp.concatenate([key_ids, key_ids], 1) == row_ids
            scores = jnp.where(same, across(qkv_ref[i, 1], own_queries, NT), MASKED)
            score_scratch[head, rows, :] = scores
            peak = jnp.maximum(peak, jnp.max(scores.reshape(16, 8, 256), 0))
        peaks.append(jnp.max(peak, 0, keepdims=True))
    scales = []
    for head in range(2):
        total = jnp.zeros((8, 256), F32)
        for i in range(8):
            rows = slice(128 * i, 128 * i + 128)
            raised = jnp.exp(score_scratch[head, rows, :] - peaks[head])
            score_scratch[head, rows, :] = raised
            total = total + jnp.sum(raised.reshape(16, 8, 256), 0)
        scales.append(1.0 / jnp.sum(total, 0, keepdims=True))
    parts = []
    for head in range(2):
        for i in range(8):
            rows = slice(128 * i, 128 * i + 128)
            weights_ref[head, rows, :] = (score_scratch[head, rows, :] * scales[head]).astype(BF16)
        mixed = across(turned_scratch[...], weights_ref[head], NN)
        parts.append(mixed[64 * head : 64 * head + 64])
    mixed = jnp.concatenate(parts, 0).T.astype(BF16)
    mixed_scratch[pl.ds(pl.multiple_of(HALO + 256 * step, 32), 256), :] = mixed

    @pl.when(step == 3)
    def _():
        for s in range(8):
            out_ref[s] = mixed_scratch[128 * s : 128 * s + WINDOW, :]


def attend(qkv, ids_row):
    return pl.pallas_call(
        attend_kernel,
        grid=(4,),
        out_shape=(
            in_hbm((8, WINDOW, 128), BF16),
            in_hbm((2, 1024, 1024), BF16),
        ),
        in_specs=[
            pl.BlockSpec((8, 3, ROWS, 128), lambda j: (0, 0, 0, 0)),
            pl.BlockSpec((1, 1024), lambda j: (0, 0)),
        ],
        out_specs=(
            pl.BlockSpec((8, WINDOW, 128), lambda j: (0, 0, 0)),
            pl.BlockSpec((2, 1024, 256), lambda j: (0, 0, j)),
        ),
        scratch_shapes=[
            pltpu.VMEM((1024, 128), F32),
            pltpu.VMEM((1024 + 2 * HALO, 128), BF16),
            pltpu.VMEM((128, 1024), BF16),
            pltpu.VMEM((2, 1024, 256), F32),
        ],
        compiler_params=pltpu.CompilerParams(
            dimension_semantics=("arbitrary",), vmem_limit_bytes=20 << 20
        ),
        name="attend",
    )(qkv, ids_row)


def tap_place(tap):
    return (tap + 1) % 8, (tap + 1) // 8 - 2


def middle_kernel(
    parity_ref,
    mixed_ref,
    stream_ref,
    cotangent_ref,
    before_ref,
    after_ref,
    ids_ref,
    attn_out_hbm,
    point_in_hbm,
    taps_ref,
    point_out_hbm,
    norm_gain_ref,
    conv_gain_ref,
    out_ref,
    keep_ref,
    send_ref,
    attn_out_ref,
    point_in_ref,
    point_out_ref,
    arrivals,
    conv_in_ref,
    moved_ref,
    grad_ref,
    grad_moved_ref,
    ids_moved_ref,
    taps_f32_ref,
    hat_ref,
    linear_ref,
    logistic_ref,
    act_grad_ref,
    activated_ref,
    in_grad_ref,
    tap_sums_ref,
):
    own = slice(HALO, HALO + ROWS)
    attn_out_copy = pltpu.make_async_copy(attn_out_hbm, attn_out_ref, arrivals.at[0])
    point_in_copy = pltpu.make_async_copy(point_in_hbm, point_in_ref, arrivals.at[1])
    point_out_copy = pltpu.make_async_copy(point_out_hbm, point_out_ref, arrivals.at[2])
    attn_out_copy.start()
    point_in_copy.start()
    point_out_copy.start()
    ids = jnp.broadcast_to(ids_ref[...], (128, 256)).T
    grad_ref[...] = jnp.zeros_like(grad_ref)
    taps_f32_ref[...] = taps_ref[...].astype(F32)
    conv_in_ref[0:8, 0:128] = jnp.zeros((8, 128), F32)
    for m in range(8):
        ids_moved_ref[m] = ids[m : m + WINDOW]

    mixed = jnp.concatenate([mixed_ref[h] for h in range(8)], 1)
    attn_out_copy.wait()
    hidden = across(mixed, attn_out_ref[...], NN)
    hidden += jnp.concatenate([before_ref[0:HALO], stream_ref[...], after_ref[0:HALO]], 0).astype(F32)
    center = jnp.mean(hidden, -1, keepdims=True)
    shifted = hidden - center
    inverse = lax.rsqrt(jnp.mean(shifted * shifted, -1, keepdims=True) + EPSILON)
    hat = shifted * inverse
    hat_ref[...] = hat[own]
    inverse_in = inverse[own]
    normed = (hat * norm_gain_ref[...]).astype(BF16)
    point_in_copy.wait()
    for c in range(4):
        cols = slice(256 * c, 256 * c + 256)
        gate_cols = slice(1024 + 256 * c, 1024 + 256 * c + 256)
        linear = across(normed, point_in_ref[:, cols], NN)
        logistic = jax.nn.sigmoid(across(normed, point_in_ref[:, gate_cols], NN))
        conv_in_ref[0:WINDOW, cols] = (linear * logistic).astype(BF16).astype(F32)
        linear_ref[:, cols] = linear[own]
        logistic_ref[:, cols] = logistic[own]

    cotangent = jnp.concatenate(
        [before_ref[HALO : 2 * HALO], cotangent_ref[...], after_ref[HALO : 2 * HALO]], 0
    )
    point_out_copy.wait()
    act_grad_ref[...] = across(cotangent, point_out_ref[...], NT)

    @pl.loop(0, 8)
    def _(block):
        cols = pl.ds(pl.multiple_of(128 * block, 128), 128)
        for m in range(8):
            moved_ref[m, 0:184, cols] = conv_in_ref[m : m + 184, cols]

    conv_gain = conv_gain_ref[...]

    def tapped(source_ref, base, weight_of):
        own_ids = ids_moved_ref[0, pl.ds(base, 8), :]
        sums = [jnp.zeros((8, 128), F32) for _ in range(8)]
        for tap in range(TAPS):
            m, a = tap_place(tap)
            rows = pl.ds(pl.multiple_of(base + 8 * a, 8), 8)
            same = ids_moved_ref[m, rows, :] == own_ids
            at = weight_of(tap)
            for block in range(8):
                cols = slice(128 * block, 128 * block + 128)
                term = jnp.where(same, source_ref[m, rows, cols], 0.0)
                sums[block] = sums[block] + term * taps_f32_ref[at : at + 1, cols]
        return jnp.concatenate(sums, 1)

    @pl.loop(0, 20)
    def _(group):
        base = pl.multiple_of(16 + 8 * group, 8)
        conv_out = tapped(moved_ref, base, lambda tap: tap)
        shifted = conv_out - jnp.mean(conv_out, -1, keepdims=True)
        inverse = lax.rsqrt(jnp.mean(shifted * shifted, -1, keepdims=True) + EPSILON)
        hat = shifted * inverse
        normed = hat * conv_gain
        logistic = jax.nn.sigmoid(normed)
        activated_ref[pl.ds(base, 8), :] = normed * logistic
        slope = logistic * (1.0 + normed * (1.0 - logistic))
        scaled = act_grad_ref[pl.ds(base, 8), :] * slope * conv_gain
        grad_ref[pl.ds(base, 8), :] = inverse * (
            scaled
            - jnp.mean(scaled, -1, keepdims=True)
            - hat * jnp.mean(scaled * hat, -1, keepdims=True)
        )

    @pl.loop(0, 8)
    def _(block):
        cols = pl.ds(pl.multiple_of(128 * block, 128), 128)
        for m in range(8):
            grad_moved_ref[m, 0:184, cols] = grad_ref[m : m + 184, cols]

    @pl.loop(0, 16)
    def _(group):
        base = pl.multiple_of(HALO + 8 * group, 8)
        in_grad_ref[pl.ds(pl.multiple_of(8 * group, 8), 8), :] = tapped(
            grad_moved_ref, base, lambda tap: 30 - tap
        )

    tap_sums_ref[31:32, :] = jnp.zeros((1, 1024), F32)
    for first in range(0, TAPS, 4):
        here = list(range(first, min(first + 4, TAPS)))

        def row_group(group, sums, here=here):
            base = pl.multiple_of(HALO + 8 * group, 8)
            own_ids = ids_moved_ref[0, pl.ds(base, 8), :]
            places = []
            for tap in here:
                m, a = tap_place(tap)
                rows = pl.ds(pl.multiple_of(base + 8 * a, 8), 8)
                places.append((m, rows, ids_moved_ref[m, rows, :] == own_ids))
            grown = []
            for block in range(8):
                cols = slice(128 * block, 128 * block + 128)
                own_grad = grad_ref[pl.ds(base, 8), cols]
                for at, (m, rows, same) in enumerate(places):
                    term = jnp.where(same, moved_ref[m, rows, cols], 0.0)
                    grown.append(sums[len(here) * block + at] + own_grad * term)
            return tuple(grown)

        sums = lax.fori_loop(
            0,
            16,
            row_group,
            tuple(jnp.zeros((8, 128), F32) for _ in range(8 * len(here))),
            unroll=4,
        )
        for at, tap in enumerate(here):
            tap_sums_ref[tap : tap + 1, :] = jnp.concatenate(
                [jnp.sum(sums[len(here) * block + at], 0, keepdims=True) for block in range(8)], 1
            )
    tap_part = tap_sums_ref[...].astype(BF16)
    keep_ref[256:288, :] = tap_part
    send_ref[256:288, :] = tap_part

    back = jnp.zeros((ROWS, 1024), F32)
    for c in range(4):
        cols = slice(256 * c, 256 * c + 256)
        gate_cols = slice(1024 + 256 * c, 1024 + 256 * c + 256)
        logistic = logistic_ref[:, cols]
        toward = in_grad_ref[:, cols] * logistic
        gate = (toward * linear_ref[:, cols] * (1.0 - logistic)).astype(BF16)
        back += across(toward.astype(BF16), point_in_ref[:, cols], NT)
        back += across(gate, point_in_ref[:, gate_cols], NT)
    scaled = back * norm_gain_ref[...]
    hat = hat_ref[...]
    stream_grad = cotangent_ref[...].astype(F32) + inverse_in * (
        scaled
        - jnp.mean(scaled, -1, keepdims=True)
        - hat * jnp.mean(scaled * hat, -1, keepdims=True)
    )
    stream_grad = stream_grad.astype(BF16)
    mixed_grad = across(stream_grad, attn_out_ref[...], NT).astype(BF16)
    for h in range(8):
        cols = slice(128 * h, 128 * h + 128)
        out_ref[h, 0:128, :] = mixed_grad[:, cols]
        out_ref[h, 128:256, :] = stream_grad[:, cols]
    activated = activated_ref[own, :].astype(BF16)
    own_mixed = mixed[own]

    @pl.when(parity_ref[0] == 0)
    def _():
        keep_ref[0:128] = own_mixed
        keep_ref[128:256] = stream_grad
        send_ref[0:128] = activated
        send_ref[128:256] = cotangent_ref[...]

    @pl.when(parity_ref[0] != 0)
    def _():
        keep_ref[0:128] = activated
        keep_ref[128:256] = cotangent_ref[...]
        send_ref[0:128] = own_mixed
        send_ref[128:256] = stream_grad


def middle(parity, *arrays):
    return pl.pallas_call(
        middle_kernel,
        out_shape=(
            in_hbm((8, 256, 128), BF16),
            in_hbm((288, 1024), BF16),
            in_hbm((288, 1024), BF16),
        ),
        in_specs=[whole(pltpu.SMEM)]
        + [whole()] * 6
        + [whole(pl.ANY), whole(pl.ANY), whole(), whole(pl.ANY), whole(), whole()],
        out_specs=(whole(), whole(), whole()),
        scratch_shapes=[
            pltpu.VMEM((1024, 1024), BF16),
            pltpu.VMEM((1024, 2048), BF16),
            pltpu.VMEM((1024, 1024), BF16),
            pltpu.SemaphoreType.DMA((3,)),
            pltpu.VMEM((WINDOW, 1024), F32),
            pltpu.VMEM((8, WINDOW, 1024), F32),
            pltpu.VMEM((WINDOW, 1024), F32),
            pltpu.VMEM((8, WINDOW, 1024), F32),
            pltpu.VMEM((8, WINDOW, 128), F32),
            pltpu.VMEM((TAPS, 1024), F32),
            pltpu.VMEM((ROWS, 1024), F32),
            pltpu.VMEM((ROWS, 1024), F32),
            pltpu.VMEM((ROWS, 1024), F32),
            pltpu.VMEM((WINDOW, 1024), F32),
            pltpu.VMEM((WINDOW, 1024), F32),
            pltpu.VMEM((ROWS, 1024), F32),
            pltpu.VMEM((32, 1024), F32),
        ],
        compiler_params=pltpu.CompilerParams(vmem_limit_bytes=40 << 20),
        name="middle",
    )(parity, *arrays)


def product_kernel(place_ref, keep_ref, received_ref, own_ref, sent_ref):
    left = jnp.concatenate([keep_ref[0:128], received_ref[0:128]], 0)
    right = jnp.concatenate([keep_ref[128:256], received_ref[128:256]], 0)
    row = lax.broadcasted_iota(jnp.int32, (1024, 128), 0)
    block = ((row & 31) >> 2) ^ place_ref[0]
    goal = 128 * block + 4 * (row >> 5) + (row & 3)
    lane = lax.broadcasted_iota(jnp.int32, (1024, 128), 1)
    for c in range(4):
        order = jnp.concatenate(
            [
                jnp.where(goal == lane + (256 * c + 128 * e), 1.0, 0.0).astype(BF16)
                for e in range(2)
            ],
            1,
        )
        ordered = across(left, order, NN).astype(BF16)
        result = across(ordered, right, TN)
        if c < 2:
            own_ref[256 * c : 256 * c + 256] = result
        else:
            sent_ref[256 * c - 512 : 256 * c - 256] = result.astype(BF16)


def product(place, keep, received):
    return pl.pallas_call(
        product_kernel,
        out_shape=(in_hbm((512, 1024), F32), in_hbm((512, 1024), BF16)),
        in_specs=[whole(pltpu.SMEM), whole(), whole()],
        out_specs=(whole(),) * 2,
        compiler_params=pltpu.CompilerParams(vmem_limit_bytes=14 << 20),
        name="product",
    )(place, keep, received)


def attend_back_kernel(
    qkv_ref, got_ref, weights_ref, out_ref, dq_ref, dk_ref, dv_ref, turned_scratch, slope_scratch, change_scratch
):
    step = pl.program_id(0)

    @pl.when(step == 0)
    def _():
        turned_scratch[...] = qkv_ref[:, 1].reshape(1024, 128).T

    queries = qkv_ref[pl.ds(2 * step, 2), 0].reshape(256, 128) * jnp.asarray(HEAD_DIM**-0.5, BF16)
    upstream = got_ref[pl.ds(2 * step, 2), 0:128].reshape(256, 128)
    own_queries = [half_of(queries, head) for head in range(2)]
    own_up = [half_of(upstream, head) for head in range(2)]
    deltas = []
    for head in range(2):
        delta = jnp.zeros((8, 256), F32)
        for i in range(8):
            rows = slice(128 * i, 128 * i + 128)
            slope = across(qkv_ref[i, 2], own_up[head], NT)
            slope_scratch[head, rows, :] = slope
            product = weights_ref[head, rows, :].astype(F32) * slope
            delta = delta + jnp.sum(product.reshape(16, 8, 256), 0)
        deltas.append(jnp.sum(delta, 0, keepdims=True))
    dq_parts = []
    for head in range(2):
        for i in range(8):
            rows = slice(128 * i, 128 * i + 128)
            wide = weights_ref[head, rows, :].astype(F32)
            change = wide * (slope_scratch[head, rows, :] - deltas[head])
            change_scratch[rows, 256 * head : 256 * head + 256] = change.astype(BF16)
        dq = across(turned_scratch[...], change_scratch[:, 256 * head : 256 * head + 256], NN)
        dq_parts.append(dq[64 * head : 64 * head + 64])
    both_weights = jnp.concatenate([weights_ref[0], weights_ref[1]], 1)
    dv_add = across(both_weights, jnp.concatenate(own_up, 0), NN)
    dk_add = across(change_scratch[...], jnp.concatenate(own_queries, 0), NN)
    dq = jnp.concatenate(dq_parts, 0).T * HEAD_DIM**-0.5
    dq_ref[pl.ds(pl.multiple_of(256 * step, 256), 256), :] = dq.astype(BF16)

    @pl.when(step == 0)
    def _():
        dk_ref[...] = dk_add
        dv_ref[...] = dv_add

    @pl.when(step != 0)
    def _():
        dk_ref[...] += dk_add
        dv_ref[...] += dv_add

    @pl.when(step == 3)
    def _():
        grads = (
            dq_ref[...].reshape(8, 128, 128),
            dk_ref[...].astype(BF16).reshape(8, 128, 128),
            dv_ref[...].astype(BF16).reshape(8, 128, 128),
            got_ref[:, 128:256, :],
        )
        for a in range(4):
            for b in range(8):
                out_ref[8 * a + b] = grads[a][:, 16 * b : 16 * b + 16, :]


def attend_back(qkv, got, weights):
    return pl.pallas_call(
        attend_back_kernel,
        grid=(4,),
        out_shape=in_hbm((32, 8, 16, 128), BF16),
        in_specs=[
            pl.BlockSpec((8, 3, ROWS, 128), lambda j: (0, 0, 0, 0)),
            pl.BlockSpec((8, 256, 128), lambda j: (0, 0, 0)),
            pl.BlockSpec((2, 1024, 256), lambda j: (0, 0, j)),
        ],
        out_specs=pl.BlockSpec((32, 8, 16, 128), lambda j: (0, 0, 0, 0)),
        scratch_shapes=[
            pltpu.VMEM((1024, 128), BF16),
            pltpu.VMEM((1024, 128), F32),
            pltpu.VMEM((1024, 128), F32),
            pltpu.VMEM((128, 1024), BF16),
            pltpu.VMEM((2, 1024, 256), F32),
            pltpu.VMEM((1024, 512), BF16),
        ],
        compiler_params=pltpu.CompilerParams(
            dimension_semantics=("arbitrary",), vmem_limit_bytes=20 << 20
        ),
        name="attend_back",
    )(qkv, got, from_hbm(weights))


def swap_kernel(plan_ref, got_ref, tail_ref, out_ref):
    @pl.loop(0, 16)
    def _(pair):
        rows = tail_ref[pl.ds(pl.multiple_of(8 * pair, 8), 8), :]
        for e in range(2):
            slot = 2 * pair + e
            source = plan_ref[slot]
            for h in range(8):
                out_ref[slot, 16 * h : 16 * h + 16, :] = got_ref[source, h]
            pieces = [rows[4 * e : 4 * e + 4, 128 * c : 128 * c + 128] for c in range(8)]
            out_ref[slot, 128:160, :] = jnp.concatenate(pieces, 0).astype(BF16)


def swap(plan, got, tail):
    return pl.pallas_call(
        swap_kernel,
        out_shape=in_hbm((32, 160, 128), BF16),
        in_specs=[whole(pltpu.SMEM), whole(), whole()],
        out_specs=whole(),
        compiler_params=pltpu.CompilerParams(vmem_limit_bytes=6 << 20),
        name="swap",
    )(plan, got, tail)


def unpack_kernel(got_ref, dq_ref, dk_ref, dv_ref, stream_ref, proj_ref):
    outs = (dq_ref, dk_ref, dv_ref, stream_ref)
    for a in range(4):
        for b in range(8):
            for h in range(8):
                outs[a][16 * b : 16 * b + 16, 128 * h : 128 * h + 128] = got_ref[
                    8 * a + b, 16 * h : 16 * h + 16, :
                ]
    for core in range(2):
        total = jnp.zeros((32, 128), F32)
        for chip in range(16):
            total += got_ref[2 * chip + core, 128:160, :].astype(F32)
        for c in range(8):
            at = 1024 * core + 128 * c
            proj_ref[:, at : at + 128] = total[4 * c : 4 * c + 4]


def unpack(got):
    rows = jax.ShapeDtypeStruct((ROWS, 1024), BF16)
    return pl.pallas_call(
        unpack_kernel,
        out_shape=(rows, rows, rows, rows, jax.ShapeDtypeStruct((4, 2048), F32)),
        in_specs=[whole()],
        out_specs=(whole(),) * 5,
        compiler_params=pltpu.CompilerParams(vmem_limit_bytes=6 << 20),
        name="unpack",
    )(got)


def spread(array, axis):
    return lax.all_to_all(array, axis, split_axis=0, concat_axis=0, tiled=True)


def along_z(device, partners):
    return (device & 17) | (partners[(device >> 1) & 7] << 1)


def add_from(taps, axis, partner):
    arrived = lax.ppermute(taps, axis, partner)
    return taps + arrived


def per_device(
    queries,
    keys,
    values,
    stream,
    cotangent,
    attn_out,
    point_in,
    kernel,
    point_out,
    norm_gain,
    conv_gain,
    segments,
    plan,
):
    queries, keys, values, stream, cotangent = (
        array[0] for array in (queries, keys, values, stream, cotangent)
    )
    slot = lax.axis_index("dp")
    place = lax.axis_index("seq")
    ids = lax.dynamic_index_in_dim(segments, slot, 0, keepdims=False).astype(F32)
    ids_window = lax.dynamic_slice_in_dim(
        jnp.pad(ids, (HALO, 256 - ROWS - HALO), constant_values=-1.0), place * ROWS, 256
    )
    before = lax.ppermute(
        jnp.concatenate([stream[-HALO:], cotangent[-HALO:]], 0),
        "seq",
        [(i, i + 1) for i in range(7)],
    )
    after = lax.ppermute(
        jnp.concatenate([stream[:HALO], cotangent[:HALO]], 0),
        "seq",
        [(i + 1, i) for i in range(7)],
    )
    qkv = spread(pack(queries, keys, values), "seq")
    mixed_heads, weights = attend(qkv, ids[None])
    mixed = spread(mixed_heads, "seq")
    outgoing, keep, send = middle(
        lax.rem(slot, 2)[None].astype(jnp.int32),
        mixed,
        stream,
        cotangent,
        before,
        after,
        ids_window[None],
        from_hbm(attn_out),
        from_hbm(point_in),
        kernel,
        from_hbm(point_out),
        norm_gain[None],
        conv_gain[None],
    )
    got = spread(outgoing, "seq")
    received = lax.ppermute(send, "dp", [(i, i ^ 1) for i in range(32)])
    taps = keep[256:288].astype(F32) + received[256:288].astype(F32)
    taps = add_from(taps, "dp", [(i, i ^ 2) for i in range(32)])
    own, sent = product(place[None].astype(jnp.int32), keep, received)
    crossed = lax.ppermute(sent, "seq", [(i, i ^ 4) for i in range(8)])
    taps = add_from(taps, "dp", [(i, along_z(i, (7, 2, 1, 4, 3, 6, 5, 0))) for i in range(32)])
    taps = add_from(taps, "dp", [(i, i ^ 16) for i in range(32)])
    first = attend_back(qkv, got, weights)
    first = spread(first.reshape(256, 16, 128), ("dp", "seq"))
    first = first.reshape(32, 8, 16, 128)
    own = own + crossed.astype(F32)
    quarters = [own[128 * k : 128 * k + 128] for k in range(4)]
    quarters = [quarters[0]] + [part.astype(BF16) for part in quarters[1:]]
    arrived = [
        lax.ppermute(quarters[k], "seq", [(i, i ^ k) for i in range(8)]) for k in (1, 2, 3)
    ]
    tail = quarters[0]
    for part in arrived:
        tail = tail + part.astype(F32)
    taps = add_from(taps, "dp", [(i, along_z(i, (3, 6, 5, 0, 7, 2, 1, 4))) for i in range(32)])

    second, taps = lax.optimization_barrier((swap(plan, first, tail), taps))
    for bit in (4, 1, 2):
        taps = add_from(taps, "seq", [(i, i ^ bit) for i in range(8)])
    second = spread(second, "dp")
    dq, dk, dv, stream_grad, proj_grads = unpack(second)
    return (dq[None], dk[None], dv[None], stream_grad[None], taps[:TAPS], proj_grads)


def solution(mesh):
    rows = P("dp", "seq", None)

    return jax.shard_map(
        per_device,
        mesh=mesh,
        in_specs=(rows,) * 5 + (P(),) * 8,
        out_specs=(rows, rows, rows, rows, P(), P(("dp", "seq"), None)),
        check_vma=False,
    )
```

```python
import jax
import jax.numpy as jnp
from jax import lax
from jax.experimental import pallas as pl
from jax.experimental.pallas import tpu as pltpu
from jax.sharding import PartitionSpec as P


HEAD_DIM = 64
EPSILON = 1e-05
MASKED = -1e30
F32 = jnp.float32
BF16 = jnp.bfloat16
HALO = 32
ROWS = 128
WINDOW = ROWS + 2 * HALO
TAPS = 31


def whole(space=pltpu.VMEM):
    return pl.BlockSpec(memory_space=space)


def in_hbm(shape, dtype):
    return pltpu.HBM(shape, dtype)


def from_hbm(array):
    return pltpu.with_memory_space_constraint(array, pltpu.HBM)


def across(left, right, dims):
    return lax.dot_general(left, right, (dims, ((), ())), preferred_element_type=F32)


NT = ((1,), (1,))
TN = ((0,), (0,))
NN = ((1,), (0,))


def half_of(matrix, head):
    lanes = lax.broadcasted_iota(jnp.int32, matrix.shape, 1)
    inside = (lanes >= head * HEAD_DIM) & (lanes < (head + 1) * HEAD_DIM)
    return jnp.where(inside, matrix, jnp.zeros_like(matrix))


def pack_kernel(q_ref, k_ref, v_ref, out_ref):
    for head in range(8):
        cols = slice(128 * head, 128 * head + 128)
        out_ref[head, 0] = q_ref[:, cols]
        out_ref[head, 1] = k_ref[:, cols]
        out_ref[head, 2] = v_ref[:, cols]


def pack(queries, keys, values):
    return pl.pallas_call(
        pack_kernel,
        out_shape=in_hbm((8, 3, ROWS, 128), BF16),
        in_specs=[whole()] * 3,
        out_specs=whole(),
        compiler_params=pltpu.CompilerParams(vmem_limit_bytes=6 << 20),
        name="pack",
    )(from_hbm(queries), from_hbm(keys), from_hbm(values))


def attend_kernel(
    qkv_ref, ids_ref, out_ref, weights_ref, id_scratch, mixed_scratch, turned_scratch, score_scratch
):
    step = pl.program_id(0)

    @pl.when(step == 0)
    def _():
        id_scratch[...] = jnp.broadcast_to(ids_ref[...], (128, 1024)).T
        mixed_scratch[0:HALO, :] = jnp.zeros((HALO, 128), BF16)
        mixed_scratch[1024 + HALO :, :] = jnp.zeros((HALO, 128), BF16)
        turned_scratch[...] = qkv_ref[:, 2].reshape(1024, 128).T

    queries = qkv_ref[pl.ds(2 * step, 2), 0].reshape(256, 128) * jnp.asarray(HEAD_DIM**-0.5, BF16)
    row_ids = ids_ref[:, pl.ds(pl.multiple_of(256 * step, 256), 256)]
    peaks = []
    for head in range(2):
        own_queries = half_of(queries, head)
        peak = jnp.full((8, 256), MASKED, F32)
        for i in range(8):
            rows = slice(128 * i, 128 * i + 128)
            key_ids = id_scratch[rows, :]
            same = jnp.concatenate([key_ids, key_ids], 1) == row_ids
            scores = jnp.where(same, across(qkv_ref[i, 1], own_queries, NT), MASKED)
            score_scratch[head, rows, :] = scores
            peak = jnp.maximum(peak, jnp.max(scores.reshape(16, 8, 256), 0))
        peaks.append(jnp.max(peak, 0, keepdims=True))
    scales = []
    for head in range(2):
        total = jnp.zeros((8, 256), F32)
        for i in range(8):
            rows = slice(128 * i, 128 * i + 128)
            raised = jnp.exp(score_scratch[head, rows, :] - peaks[head])
            score_scratch[head, rows, :] = raised
            total = total + jnp.sum(raised.reshape(16, 8, 256), 0)
        scales.append(1.0 / jnp.sum(total, 0, keepdims=True))
    parts = []
    for head in range(2):
        for i in range(8):
            rows = slice(128 * i, 128 * i + 128)
            weights_ref[head, rows, :] = (score_scratch[head, rows, :] * scales[head]).astype(BF16)
        mixed = across(turned_scratch[...], weights_ref[head], NN)
        parts.append(mixed[64 * head : 64 * head + 64])
    mixed = jnp.concatenate(parts, 0).T.astype(BF16)
    mixed_scratch[pl.ds(pl.multiple_of(HALO + 256 * step, 32), 256), :] = mixed

    @pl.when(step == 3)
    def _():
        for s in range(8):
            out_ref[s] = mixed_scratch[128 * s : 128 * s + WINDOW, :]


def attend(qkv, ids_row):
    return pl.pallas_call(
        attend_kernel,
        grid=(4,),
        out_shape=(
            in_hbm((8, WINDOW, 128), BF16),
            in_hbm((2, 1024, 1024), BF16),
        ),
        in_specs=[
            pl.BlockSpec((8, 3, ROWS, 128), lambda j: (0, 0, 0, 0)),
            pl.BlockSpec((1, 1024), lambda j: (0, 0)),
        ],
        out_specs=(
            pl.BlockSpec((8, WINDOW, 128), lambda j: (0, 0, 0)),
            pl.BlockSpec((2, 1024, 256), lambda j: (0, 0, j)),
        ),
        scratch_shapes=[
            pltpu.VMEM((1024, 128), F32),
            pltpu.VMEM((1024 + 2 * HALO, 128), BF16),
            pltpu.VMEM((128, 1024), BF16),
            pltpu.VMEM((2, 1024, 256), F32),
        ],
        compiler_params=pltpu.CompilerParams(
            dimension_semantics=("arbitrary",), vmem_limit_bytes=20 << 20
        ),
        name="attend",
    )(qkv, ids_row)


def tap_place(tap):
    return (tap + 1) % 8, (tap + 1) // 8 - 2


def prepare_kernel(
    cotangent_ref,
    before_ref,
    after_ref,
    ids_ref,
    point_out_ref,
    taps_ref,
    act_grad_ref,
    ids_moved_ref,
    taps_f32_ref,
):
    taps_f32_ref[...] = taps_ref[...].astype(F32)
    ids = jnp.broadcast_to(ids_ref[...], (128, 256)).T
    for m in range(8):
        ids_moved_ref[m] = ids[m : m + WINDOW]
    cotangent = jnp.concatenate(
        [before_ref[HALO : 2 * HALO], cotangent_ref[...], after_ref[HALO : 2 * HALO]], 0
    )
    act_grad_ref[...] = across(cotangent, point_out_ref[...], NT)


def prepare(*arrays):
    return pl.pallas_call(
        prepare_kernel,
        out_shape=(
            jax.ShapeDtypeStruct((WINDOW, 1024), F32),
            jax.ShapeDtypeStruct((8, WINDOW, 128), F32),
            in_hbm((TAPS, 1024), F32),
        ),
        in_specs=[whole()] * 6,
        out_specs=(whole(),) * 3,
        compiler_params=pltpu.CompilerParams(vmem_limit_bytes=12 << 20),
        name="prepare",
    )(*arrays)


def middle_kernel(
    parity_ref,
    mixed_ref,
    stream_ref,
    cotangent_ref,
    before_ref,
    after_ref,
    act_grad_ref,
    ids_moved_ref,
    attn_out_hbm,
    point_in_hbm,
    taps_f32_ref,
    norm_gain_ref,
    conv_gain_ref,
    out_ref,
    keep_ref,
    send_ref,
    attn_out_ref,
    point_in_ref,
    arrivals,
    conv_in_ref,
    moved_ref,
    grad_ref,
    grad_moved_ref,
    hat_ref,
    linear_ref,
    logistic_ref,
    activated_ref,
    in_grad_ref,
    tap_sums_ref,
):
    own = slice(HALO, HALO + ROWS)
    attn_out_copy = pltpu.make_async_copy(attn_out_hbm, attn_out_ref, arrivals.at[0])
    point_in_copy = pltpu.make_async_copy(point_in_hbm, point_in_ref, arrivals.at[1])
    attn_out_copy.start()
    point_in_copy.start()
    grad_ref[...] = jnp.zeros_like(grad_ref)
    conv_in_ref[0:8, 0:128] = jnp.zeros((8, 128), F32)

    mixed = jnp.concatenate([mixed_ref[h] for h in range(8)], 1)
    attn_out_copy.wait()
    hidden = across(mixed, attn_out_ref[...], NN)
    hidden += jnp.concatenate([before_ref[0:HALO], stream_ref[...], after_ref[0:HALO]], 0).astype(F32)
    center = jnp.mean(hidden, -1, keepdims=True)
    shifted = hidden - center
    inverse = lax.rsqrt(jnp.mean(shifted * shifted, -1, keepdims=True) + EPSILON)
    hat = shifted * inverse
    hat_ref[...] = hat[own]
    inverse_in = inverse[own]
    normed = (hat * norm_gain_ref[...]).astype(BF16)
    point_in_copy.wait()
    for c in range(4):
        cols = slice(256 * c, 256 * c + 256)
        gate_cols = slice(1024 + 256 * c, 1024 + 256 * c + 256)
        linear = across(normed, point_in_ref[:, cols], NN)
        logistic = jax.nn.sigmoid(across(normed, point_in_ref[:, gate_cols], NN))
        conv_in_ref[0:WINDOW, cols] = (linear * logistic).astype(BF16).astype(F32)
        linear_ref[:, cols] = linear[own]
        logistic_ref[:, cols] = logistic[own]

    @pl.loop(0, 8)
    def _(block):
        cols = pl.ds(pl.multiple_of(128 * block, 128), 128)
        for m in range(8):
            moved_ref[m, 0:184, cols] = conv_in_ref[m : m + 184, cols]

    conv_gain = conv_gain_ref[...]

    def tapped(source_ref, base, weight_of):
        own_ids = ids_moved_ref[0, pl.ds(base, 8), :]
        sums = [jnp.zeros((8, 128), F32) for _ in range(8)]
        for tap in range(TAPS):
            m, a = tap_place(tap)
            rows = pl.ds(pl.multiple_of(base + 8 * a, 8), 8)
            same = ids_moved_ref[m, rows, :] == own_ids
            at = weight_of(tap)
            for block in range(8):
                cols = slice(128 * block, 128 * block + 128)
                term = jnp.where(same, source_ref[m, rows, cols], 0.0)
                sums[block] = sums[block] + term * taps_f32_ref[at : at + 1, cols]
        return jnp.concatenate(sums, 1)

    @pl.loop(0, 20)
    def _(group):
        base = pl.multiple_of(16 + 8 * group, 8)
        conv_out = tapped(moved_ref, base, lambda tap: tap)
        shifted = conv_out - jnp.mean(conv_out, -1, keepdims=True)
        inverse = lax.rsqrt(jnp.mean(shifted * shifted, -1, keepdims=True) + EPSILON)
        hat = shifted * inverse
        normed = hat * conv_gain
        logistic = jax.nn.sigmoid(normed)
        activated_ref[pl.ds(base, 8), :] = normed * logistic
        slope = logistic * (1.0 + normed * (1.0 - logistic))
        scaled = act_grad_ref[pl.ds(base, 8), :] * slope * conv_gain
        grad_ref[pl.ds(base, 8), :] = inverse * (
            scaled
            - jnp.mean(scaled, -1, keepdims=True)
            - hat * jnp.mean(scaled * hat, -1, keepdims=True)
        )

    @pl.loop(0, 8)
    def _(block):
        cols = pl.ds(pl.multiple_of(128 * block, 128), 128)
        for m in range(8):
            grad_moved_ref[m, 0:184, cols] = grad_ref[m : m + 184, cols]

    @pl.loop(0, 16)
    def _(group):
        base = pl.multiple_of(HALO + 8 * group, 8)
        in_grad_ref[pl.ds(pl.multiple_of(8 * group, 8), 8), :] = tapped(
            grad_moved_ref, base, lambda tap: 30 - tap
        )

    tap_sums_ref[31:32, :] = jnp.zeros((1, 1024), F32)
    for first in range(0, TAPS, 4):
        here = list(range(first, min(first + 4, TAPS)))

        def row_group(group, sums, here=here):
            base = pl.multiple_of(HALO + 8 * group, 8)
            own_ids = ids_moved_ref[0, pl.ds(base, 8), :]
            places = []
            for tap in here:
                m, a = tap_place(tap)
                rows = pl.ds(pl.multiple_of(base + 8 * a, 8), 8)
                places.append((m, rows, ids_moved_ref[m, rows, :] == own_ids))
            grown = []
            for block in range(8):
                cols = slice(128 * block, 128 * block + 128)
                own_grad = grad_ref[pl.ds(base, 8), cols]
                for at, (m, rows, same) in enumerate(places):
                    term = jnp.where(same, moved_ref[m, rows, cols], 0.0)
                    grown.append(sums[len(here) * block + at] + own_grad * term)
            return tuple(grown)

        sums = lax.fori_loop(
            0,
            16,
            row_group,
            tuple(jnp.zeros((8, 128), F32) for _ in range(8 * len(here))),
            unroll=2,
        )
        for at, tap in enumerate(here):
            tap_sums_ref[tap : tap + 1, :] = jnp.concatenate(
                [jnp.sum(sums[len(here) * block + at], 0, keepdims=True) for block in range(8)], 1
            )
    tap_part = tap_sums_ref[...].astype(BF16)
    keep_ref[256:288, :] = tap_part
    send_ref[256:288, :] = tap_part

    back = jnp.zeros((ROWS, 1024), F32)
    for c in range(4):
        cols = slice(256 * c, 256 * c + 256)
        gate_cols = slice(1024 + 256 * c, 1024 + 256 * c + 256)
        logistic = logistic_ref[:, cols]
        toward = in_grad_ref[:, cols] * logistic
        gate = (toward * linear_ref[:, cols] * (1.0 - logistic)).astype(BF16)
        back += across(toward.astype(BF16), point_in_ref[:, cols], NT)
        back += across(gate, point_in_ref[:, gate_cols], NT)
    scaled = back * norm_gain_ref[...]
    hat = hat_ref[...]
    stream_grad = cotangent_ref[...].astype(F32) + inverse_in * (
        scaled
        - jnp.mean(scaled, -1, keepdims=True)
        - hat * jnp.mean(scaled * hat, -1, keepdims=True)
    )
    stream_grad = stream_grad.astype(BF16)
    mixed_grad = across(stream_grad, attn_out_ref[...], NT).astype(BF16)
    for h in range(8):
        cols = slice(128 * h, 128 * h + 128)
        out_ref[h, 0:128, :] = mixed_grad[:, cols]
        out_ref[h, 128:256, :] = stream_grad[:, cols]
    activated = activated_ref[own, :].astype(BF16)
    own_mixed = mixed[own]

    @pl.when(parity_ref[0] == 0)
    def _():
        keep_ref[0:128] = own_mixed
        keep_ref[128:256] = stream_grad
        send_ref[0:128] = activated
        send_ref[128:256] = cotangent_ref[...]

    @pl.when(parity_ref[0] != 0)
    def _():
        keep_ref[0:128] = activated
        keep_ref[128:256] = cotangent_ref[...]
        send_ref[0:128] = own_mixed
        send_ref[128:256] = stream_grad


def middle(parity, *arrays):
    return pl.pallas_call(
        middle_kernel,
        out_shape=(
            in_hbm((8, 256, 128), BF16),
            in_hbm((288, 1024), BF16),
            in_hbm((288, 1024), BF16),
        ),
        in_specs=[whole(pltpu.SMEM)]
        + [whole()] * 7
        + [whole(pl.ANY), whole(pl.ANY), whole(), whole(), whole()],
        out_specs=(whole(), whole(), whole()),
        scratch_shapes=[
            pltpu.VMEM((1024, 1024), BF16),
            pltpu.VMEM((1024, 2048), BF16),
            pltpu.SemaphoreType.DMA((2,)),
            pltpu.VMEM((WINDOW, 1024), F32),
            pltpu.VMEM((8, WINDOW, 1024), F32),
            pltpu.VMEM((WINDOW, 1024), F32),
            pltpu.VMEM((8, WINDOW, 1024), F32),
            pltpu.VMEM((ROWS, 1024), F32),
            pltpu.VMEM((ROWS, 1024), F32),
            pltpu.VMEM((ROWS, 1024), F32),
            pltpu.VMEM((WINDOW, 1024), F32),
            pltpu.VMEM((ROWS, 1024), F32),
            pltpu.VMEM((32, 1024), F32),
        ],
        compiler_params=pltpu.CompilerParams(vmem_limit_bytes=40 << 20),
        name="middle",
    )(parity, *arrays)


def product_kernel(place_ref, keep_ref, received_ref, own_ref, sent_ref):
    left = jnp.concatenate([keep_ref[0:128], received_ref[0:128]], 0)
    right = jnp.concatenate([keep_ref[128:256], received_ref[128:256]], 0)
    row = lax.broadcasted_iota(jnp.int32, (1024, 128), 0)
    block = ((row & 31) >> 2) ^ place_ref[0]
    goal = 128 * block + 4 * (row >> 5) + (row & 3)
    lane = lax.broadcasted_iota(jnp.int32, (1024, 128), 1)
    for c in range(4):
        order = jnp.concatenate(
            [
                jnp.where(goal == lane + (256 * c + 128 * e), 1.0, 0.0).astype(BF16)
                for e in range(2)
            ],
            1,
        )
        ordered = across(left, order, NN).astype(BF16)
        result = across(ordered, right, TN)
        if c < 2:
            own_ref[256 * c : 256 * c + 256] = result
        else:
            sent_ref[256 * c - 512 : 256 * c - 256] = result.astype(BF16)


def product(place, keep, received):
    return pl.pallas_call(
        product_kernel,
        out_shape=(in_hbm((512, 1024), F32), in_hbm((512, 1024), BF16)),
        in_specs=[whole(pltpu.SMEM), whole(), whole()],
        out_specs=(whole(),) * 2,
        compiler_params=pltpu.CompilerParams(vmem_limit_bytes=14 << 20),
        name="product",
    )(place, keep, received)


def attend_back_kernel(
    qkv_ref, got_ref, weights_ref, out_ref, dq_ref, dk_ref, dv_ref, turned_scratch, slope_scratch, change_scratch
):
    step = pl.program_id(0)

    @pl.when(step == 0)
    def _():
        turned_scratch[...] = qkv_ref[:, 1].reshape(1024, 128).T

    queries = qkv_ref[pl.ds(2 * step, 2), 0].reshape(256, 128) * jnp.asarray(HEAD_DIM**-0.5, BF16)
    upstream = got_ref[pl.ds(2 * step, 2), 0:128].reshape(256, 128)
    own_queries = [half_of(queries, head) for head in range(2)]
    own_up = [half_of(upstream, head) for head in range(2)]
    deltas = []
    for head in range(2):
        delta = jnp.zeros((8, 256), F32)
        for i in range(8):
            rows = slice(128 * i, 128 * i + 128)
            slope = across(qkv_ref[i, 2], own_up[head], NT)
            slope_scratch[head, rows, :] = slope
            product = weights_ref[head, rows, :].astype(F32) * slope
            delta = delta + jnp.sum(product.reshape(16, 8, 256), 0)
        deltas.append(jnp.sum(delta, 0, keepdims=True))
    dq_parts = []
    for head in range(2):
        for i in range(8):
            rows = slice(128 * i, 128 * i + 128)
            wide = weights_ref[head, rows, :].astype(F32)
            change = wide * (slope_scratch[head, rows, :] - deltas[head])
            change_scratch[rows, 256 * head : 256 * head + 256] = change.astype(BF16)
        dq = across(turned_scratch[...], change_scratch[:, 256 * head : 256 * head + 256], NN)
        dq_parts.append(dq[64 * head : 64 * head + 64])
    both_weights = jnp.concatenate([weights_ref[0], weights_ref[1]], 1)
    dv_add = across(both_weights, jnp.concatenate(own_up, 0), NN)
    dk_add = across(change_scratch[...], jnp.concatenate(own_queries, 0), NN)
    dq = jnp.concatenate(dq_parts, 0).T * HEAD_DIM**-0.5
    dq_ref[pl.ds(pl.multiple_of(256 * step, 256), 256), :] = dq.astype(BF16)

    @pl.when(step == 0)
    def _():
        dk_ref[...] = dk_add
        dv_ref[...] = dv_add

    @pl.when(step != 0)
    def _():
        dk_ref[...] += dk_add
        dv_ref[...] += dv_add

    @pl.when(step == 3)
    def _():
        grads = (
            dq_ref[...].reshape(8, 128, 128),
            dk_ref[...].astype(BF16).reshape(8, 128, 128),
            dv_ref[...].astype(BF16).reshape(8, 128, 128),
            got_ref[:, 128:256, :],
        )
        for a in range(4):
            for b in range(8):
                out_ref[8 * a + b] = grads[a][:, 16 * b : 16 * b + 16, :]


def attend_back(qkv, got, weights):
    return pl.pallas_call(
        attend_back_kernel,
        grid=(4,),
        out_shape=in_hbm((32, 8, 16, 128), BF16),
        in_specs=[
            pl.BlockSpec((8, 3, ROWS, 128), lambda j: (0, 0, 0, 0)),
            pl.BlockSpec((8, 256, 128), lambda j: (0, 0, 0)),
            pl.BlockSpec((2, 1024, 256), lambda j: (0, 0, j)),
        ],
        out_specs=pl.BlockSpec((32, 8, 16, 128), lambda j: (0, 0, 0, 0)),
        scratch_shapes=[
            pltpu.VMEM((1024, 128), BF16),
            pltpu.VMEM((1024, 128), F32),
            pltpu.VMEM((1024, 128), F32),
            pltpu.VMEM((128, 1024), BF16),
            pltpu.VMEM((2, 1024, 256), F32),
            pltpu.VMEM((1024, 512), BF16),
        ],
        compiler_params=pltpu.CompilerParams(
            dimension_semantics=("arbitrary",), vmem_limit_bytes=20 << 20
        ),
        name="attend_back",
    )(qkv, got, from_hbm(weights))


def swap_kernel(plan_ref, got_ref, tail_ref, out_ref):
    @pl.loop(0, 16)
    def _(pair):
        rows = tail_ref[pl.ds(pl.multiple_of(8 * pair, 8), 8), :]
        for e in range(2):
            slot = 2 * pair + e
            source = plan_ref[slot]
            for h in range(8):
                out_ref[slot, 16 * h : 16 * h + 16, :] = got_ref[source, h]
            pieces = [rows[4 * e : 4 * e + 4, 128 * c : 128 * c + 128] for c in range(8)]
            out_ref[slot, 128:160, :] = jnp.concatenate(pieces, 0).astype(BF16)


def swap(plan, got, tail):
    return pl.pallas_call(
        swap_kernel,
        out_shape=in_hbm((32, 160, 128), BF16),
        in_specs=[whole(pltpu.SMEM), whole(), whole()],
        out_specs=whole(),
        compiler_params=pltpu.CompilerParams(vmem_limit_bytes=6 << 20),
        name="swap",
    )(plan, got, tail)


def unpack_kernel(got_ref, dq_ref, dk_ref, dv_ref, stream_ref, proj_ref):
    outs = (dq_ref, dk_ref, dv_ref, stream_ref)
    for a in range(4):
        for b in range(8):
            for h in range(8):
                outs[a][16 * b : 16 * b + 16, 128 * h : 128 * h + 128] = got_ref[
                    8 * a + b, 16 * h : 16 * h + 16, :
                ]
    for core in range(2):
        total = jnp.zeros((32, 128), F32)
        for chip in range(16):
            total += got_ref[2 * chip + core, 128:160, :].astype(F32)
        for c in range(8):
            at = 1024 * core + 128 * c
            proj_ref[:, at : at + 128] = total[4 * c : 4 * c + 4]


def unpack(got):
    rows = jax.ShapeDtypeStruct((ROWS, 1024), BF16)
    return pl.pallas_call(
        unpack_kernel,
        out_shape=(rows, rows, rows, rows, jax.ShapeDtypeStruct((4, 2048), F32)),
        in_specs=[whole()],
        out_specs=(whole(),) * 5,
        compiler_params=pltpu.CompilerParams(vmem_limit_bytes=6 << 20),
        name="unpack",
    )(got)


def spread(array, axis):
    return lax.all_to_all(array, axis, split_axis=0, concat_axis=0, tiled=True)


def along_z(device, partners):
    return (device & 17) | (partners[(device >> 1) & 7] << 1)


def add_from(taps, axis, partner, narrow=False):
    sent = taps.astype(BF16) if narrow else taps
    arrived = lax.ppermute(sent, axis, partner)
    return sent.astype(F32) + arrived.astype(F32)


def per_device(
    queries,
    keys,
    values,
    stream,
    cotangent,
    attn_out,
    point_in,
    kernel,
    point_out,
    norm_gain,
    conv_gain,
    segments,
    plan,
):
    queries, keys, values, stream, cotangent = (
        array[0] for array in (queries, keys, values, stream, cotangent)
    )
    slot = lax.axis_index("dp")
    place = lax.axis_index("seq")
    ids = lax.dynamic_index_in_dim(segments, slot, 0, keepdims=False).astype(F32)
    ids_window = lax.dynamic_slice_in_dim(
        jnp.pad(ids, (HALO, 256 - ROWS - HALO), constant_values=-1.0), place * ROWS, 256
    )
    before = lax.ppermute(
        jnp.concatenate([stream[-HALO:], cotangent[-HALO:]], 0),
        "seq",
        [(i, i + 1) for i in range(7)],
    )
    after = lax.ppermute(
        jnp.concatenate([stream[:HALO], cotangent[:HALO]], 0),
        "seq",
        [(i + 1, i) for i in range(7)],
    )
    qkv = spread(pack(queries, keys, values), "seq")
    mixed_heads, weights = attend(qkv, ids[None])
    mixed = spread(mixed_heads, "seq")
    act_grad, ids_moved, taps_wide = prepare(
        cotangent, before, after, ids_window[None], from_hbm(point_out), from_hbm(kernel)
    )
    outgoing, keep, send = middle(
        lax.rem(slot, 2)[None].astype(jnp.int32),
        mixed,
        stream,
        cotangent,
        before,
        after,
        act_grad,
        ids_moved,
        from_hbm(attn_out),
        from_hbm(point_in),
        from_hbm(taps_wide),
        norm_gain[None],
        conv_gain[None],
    )
    got = spread(outgoing, "seq")
    received = lax.ppermute(send, "dp", [(i, i ^ 1) for i in range(32)])
    taps = keep[256:288].astype(F32) + received[256:288].astype(F32)
    taps = add_from(taps, "dp", [(i, i ^ 2) for i in range(32)])
    own, sent = product(place[None].astype(jnp.int32), keep, received)
    crossed = lax.ppermute(sent, "seq", [(i, i ^ 4) for i in range(8)])
    taps = add_from(taps, "dp", [(i, along_z(i, (7, 2, 1, 4, 3, 6, 5, 0))) for i in range(32)])
    taps = add_from(taps, "dp", [(i, i ^ 16) for i in range(32)])
    first = attend_back(qkv, got, weights)
    first = spread(first.reshape(256, 16, 128), ("dp", "seq"))
    first = first.reshape(32, 8, 16, 128)
    own = own + crossed.astype(F32)
    quarters = [own[128 * k : 128 * k + 128] for k in range(4)]
    quarters = [quarters[0]] + [part.astype(BF16) for part in quarters[1:]]
    arrived = [
        lax.ppermute(quarters[k], "seq", [(i, i ^ k) for i in range(8)]) for k in (1, 2, 3)
    ]
    tail = quarters[0]
    for part in arrived:
        tail = tail + part.astype(F32)
    taps = add_from(taps, "dp", [(i, along_z(i, (3, 6, 5, 0, 7, 2, 1, 4))) for i in range(32)], True)

    second, taps = lax.optimization_barrier((swap(plan, first, tail), taps))
    for bit in (4, 1, 2):
        taps = add_from(taps, "seq", [(i, i ^ bit) for i in range(8)])
    second = spread(second, "dp")
    dq, dk, dv, stream_grad, proj_grads = unpack(second)
    return (dq[None], dk[None], dv[None], stream_grad[None], taps[:TAPS], proj_grads)


def solution(mesh):
    rows = P("dp", "seq", None)

    return jax.shard_map(
        per_device,
        mesh=mesh,
        in_specs=(rows,) * 5 + (P(),) * 8,
        out_specs=(rows, rows, rows, rows, P(), P(("dp", "seq"), None)),
        check_vma=False,
    )
```
